32 devices in a mesh: groups: 2 (over x), net: 8 (over z, y), tm: 2 (over core).
Axes of the slice: x: 2, y: 2, z: 4, core: 2. Of those that a mesh axis runs over, the one named last changes fastest.
Arguments:
- proposal: float32 [16384, 256], P(('groups', 'net'), 'tm'), parts along dimension 0, may hold values from -6 to 6
- flow_dual: float32 [8192, 256], P(('groups', 'net'), 'tm'), parts along dimension 0, may hold values from -4 to 4
- shift_factors: bfloat16 [4096, 8192], P('net'), may hold values from -0.09375 to 0.09375
- outage_line: int32 [4096], P('net'), may hold values from 0 to 511
- ratings: float32 [512], replicated, may hold values from 0.3 to 3
- ramp_limit: float32 [8192], P('net'), may hold values from 0.05 to 1
Outputs:
- dispatch: float32 [16384, 256], P(('groups', 'net'), 'tm'), parts along dimension 0
- new_dual: float32 [8192, 256], P(('groups', 'net'), 'tm'), parts along dimension 0
- residual_norms: float32 [4], P('groups'), parts along dimension 0
The draws below stay inside these ranges and needn't reach their ends.
There are 2 independent parts, one for each index of `groups`. The reference program is written for one: setup_inputs(seed, part) draws one part's arguments, and reference() takes and returns one part's arrays. A program takes and returns all parts, laid end to end along the dimension named above; an argument that names none is the same for every part. Nothing has to cross between parts.
All inputs are finite; a program needn't handle non-finite values.
Results may differ from the reference program's by a relative error of at most 0.0024.
Values may be sent and summed in bfloat16 or wider, within the bound.
No kernel may reach another device: no remote copies, remote signals or barrier semaphores. Data moves between devices by JAX's collectives and lax.ppermute only.
A program may use at most 64 MiB of HBM per device.

```python
import math
import jax
import jax.numpy as jnp
from jax import lax

NB = 8192
NOUT = 512
PASSES = 2
L = 4096
T_SIZE = 256


def touch_ends(drawn, rng, smallest, high):
    spot = [jax.random.randint(jax.random.fold_in(rng, axis), (), 0, length) for axis, length in enumerate(drawn.shape)]
    widest = drawn.shape.index(max(drawn.shape))
    beside = spot[:widest] + [(spot[widest] + 1) % drawn.shape[widest]] + spot[widest + 1:]
    return drawn.at[tuple(spot)].set(smallest).at[tuple(beside)].set(high)


def with_spikes(entries, own_key, source, target, parts, factor):
    def block_of(axis_at):
        return (jnp.arange(entries.shape[axis_at]) // (entries.shape[axis_at] // parts)).reshape((-1,) + (1,) * (entries.ndim - 1 - axis_at))

    near = jax.random.permutation(own_key, parts)[block_of(target)]
    far = (block_of(target) + parts // 2) % parts
    return jnp.where((block_of(source) == near) | (block_of(source) == far), factor * entries, entries)


def level_of(stream_key, dims, cuts, smallest, high):
    def one(dim, blocks):
        draws = jax.random.uniform(jax.random.fold_in(jax.random.fold_in(stream_key, 6), dim), (blocks,), jnp.float32, smallest / len(cuts), high / len(cuts))
        return jnp.repeat(jnp.exp(draws), dims[dim] // blocks).reshape((-1,) + (1,) * (len(dims) - dim - 1))

    gain = one(*cuts[0])
    for cut in cuts[1:]:
        gain = gain * one(*cut)
    return gain


def gaussian(stream_key, dims, scale, most, shards=(), kind=jnp.bfloat16):
    result = scale * jax.random.normal(stream_key, dims, jnp.float32)
    if shards:
        result = result * level_of(stream_key, dims, shards, -0.22, 0.18)
    return jnp.clip(result, -most, most).astype(kind)


def noise_with(own_key, shape, scale, most, shards, heavy, kind=jnp.bfloat16):
    entries = scale * jax.random.normal(own_key, shape, jnp.float32)
    if shards:
        entries = entries * level_of(own_key, shape, shards, -0.22, 0.18)
    return jnp.clip(with_spikes(entries, jax.random.fold_in(own_key, 3), *heavy), -most, most).astype(kind)


def setup_inputs(seed: int = 0, part: int = 0) -> dict:
    arg_keys = jax.random.split(jax.random.key(seed), 7)
    own_keys = jax.random.split(jax.random.fold_in(arg_keys[6], part), 7)
    return {
        "proposal": gaussian(own_keys[0], (NB, T_SIZE), 1.0, 6.0, ((0, 8), (1, 2)), jnp.float32),
        "flow_dual": gaussian(own_keys[1], (L, T_SIZE), 0.5, 4.0, ((0, 8), (1, 2)), jnp.float32),
        "shift_factors": noise_with(arg_keys[2], (L, NB), NB ** -0.5, 0.09375, ((0, 8),), (0, 1, 8, 2.0)),
        "outage_line": touch_ends(jax.random.randint(arg_keys[3], (L,), 0, NOUT), jax.random.fold_in(arg_keys[3], 1), 0, NOUT - 1).astype(jnp.int32),
        "ratings": jnp.clip(jnp.exp(jax.random.uniform(arg_keys[4], (NOUT,), jnp.float32, math.log(0.3), math.log(3.0))), 0.3, 3.0),
        "ramp_limit": jnp.clip(jnp.exp(math.log(1.0) - 2.9957323 * jax.random.uniform(arg_keys[5], (NB,), jnp.float32) ** level_of(arg_keys[5], (NB,), ((0, 8),), -0.2, 0.2)), 0.05, 1.0),
    }


def reference(proposal, flow_dual, shift_factors, outage_line, ratings, ramp_limit):
    limits = ratings[outage_line][:, None]
    inject = proposal
    dual = flow_dual
    sums = []
    for pass_idx in range(PASSES):
        flows = jnp.dot(shift_factors, inject.astype(jnp.bfloat16), preferred_element_type=jnp.float32)
        kept = jnp.clip(flows + dual, -limits, limits)
        misfit = flows - kept
        dual = dual + misfit
        sums.append(jnp.sum(misfit * misfit))
        spread = lax.dot_general(shift_factors, misfit.astype(jnp.bfloat16), (((0,), (0,)), ((), ())), preferred_element_type=jnp.float32)
        inject = inject - 0.1 * spread
    count = jnp.float32(L * T_SIZE)
    residual_norms = jnp.sqrt(jnp.stack(sums) / count)
    bound = ramp_limit[:, None]
    step = inject[:, 1:] - inject[:, :-1]
    excess = step - jnp.clip(step, -bound, bound)
    zeros = jnp.zeros((inject.shape[0], 1), jnp.float32)
    excess = jnp.concatenate([zeros, excess, zeros], axis=1)
    dispatch = inject - 0.5 * excess[:, :-1] + 0.5 * excess[:, 1:]
    return (dispatch, dual, residual_norms)
```

```python
import jax
import jax.numpy as jnp
from jax import lax
from jax.experimental import pallas as pl
from jax.experimental.pallas import tpu as pltpu
from jax.sharding import PartitionSpec as P

relax_step = 0.1
chunks = 2
passes = 2
longest_ring = 8


def ring_order(count):
    return list(range(0, count, 2)) + list(range(count - 1 - count % 2, 0, -2))


def hop_counts(count, chunk):
    far, near = count // 2, (count - 1) // 2
    return (near, far) if chunk % 2 else (far, near)


def gather_sends(count):
    sends = []
    for hop in range(1, count // 2 + 1):
        for flip in (0, 1):
            for chunk in range(chunks):
                for way in (1, -1):
                    limit = hop_counts(count, chunk)[0 if way == 1 else 1]
                    if hop <= limit and (chunk % 2 == (way == -1)) == (flip == 0):
                        sends.append((chunk, way, hop))
    return sends


def hop_to(block, send, order):
    count = len(order)
    pairs = [(order[i], order[(i + send[1]) % count]) for i in range(count)]
    return lax.ppermute(block, "net", pairs)


def by_distance(count):
    out = [0]
    for hop in range(1, count // 2 + 1):
        out += [count - hop] if 2 * hop == count else [count - hop, hop]
    return out


def ring_gather(pieces, order):
    count = len(order)
    got = [{0: p} for p in pieces]
    held = {}
    for send in gather_sends(count):
        chunk, way, hop = send
        block = hop_to(held.get((chunk, way), pieces[chunk]), send, order)
        held[chunk, way] = block
        got[chunk][(-way * hop) % count] = block
    return got


def ring_scatter(part, order):
    count = len(order)
    held = {}
    for send in reversed(gather_sends(count)):
        chunk, way, hop = send
        mine = part[chunk][(way * hop) % count]
        if (chunk, way) in held:
            mine = mine + held[chunk, way].astype(jnp.float32)
        held[chunk, way] = hop_to(mine.astype(jnp.bfloat16), send, order)
    totals = []
    for chunk in range(chunks):
        total = part[chunk][0]
        for way in (1, -1):
            if (chunk, way) in held:
                total = total + held[chunk, way].astype(jnp.float32)
        totals.append(total)
    return totals


def reorder_kernel(at_ref, factors_ref, out_ref, sems):
    width = out_ref.shape[1] // sems.shape[0]
    copies = [
        pltpu.make_async_copy(
            factors_ref.at[:, pl.ds(pl.multiple_of(at_ref[j] * width, width), width)],
            out_ref.at[:, pl.ds(j * width, width)],
            sems.at[j],
        )
        for j in range(sems.shape[0])
    ]
    for copy in copies:
        copy.start()
    for copy in copies:
        copy.wait()


def reorder(factors, at):
    return pl.pallas_call(
        reorder_kernel,
        out_shape=jax.ShapeDtypeStruct(factors.shape, factors.dtype),
        in_specs=[pl.BlockSpec(memory_space=pltpu.SMEM), pl.BlockSpec(memory_space=pl.ANY)],
        out_specs=pl.BlockSpec(memory_space=pltpu.VMEM),
        scratch_shapes=[pltpu.SemaphoreType.DMA((at.shape[0],))],
        compiler_params=pltpu.CompilerParams(vmem_limit_bytes=20 << 20),
        cost_estimate=pl.CostEstimate(flops=0, transcendentals=0, bytes_accessed=2 * factors.size * factors.dtype.itemsize),
    )(at, factors)


def limits_of(outage_line, ratings):
    levels = lax.broadcasted_iota(jnp.int32, (outage_line.shape[0], ratings.shape[0]), 1)
    return jnp.sum(jnp.where(outage_line[:, None] == levels, ratings[None, :], 0.0), axis=1)


def project(flows, dual, limits):
    bound = limits[:, None]
    kept = jnp.clip(flows + dual, -bound, bound)
    misfit = flows - kept
    return (misfit, dual + misfit)


def total_over(value, axis):
    count = lax.axis_size(axis)
    if count & (count - 1):
        return lax.psum(value, axis)
    bit = 1
    while bit < count:
        value = value + lax.ppermute(value, axis, [(i, i ^ bit) for i in range(count)])
        bit *= 2
    return value


def beside(block, axis):
    count = lax.axis_size(axis)
    first, last = block[:, :1], block[:, -1:]
    zeros = jnp.zeros_like(first)
    if count == 1:
        return zeros, zeros
    if count == 2:
        at = lax.axis_index(axis)
        other = lax.ppermute(jnp.where(at == 0, last, first), axis, [(0, 1), (1, 0)])
        return jnp.where(at == 0, zeros, other), jnp.where(at == 0, other, zeros)
    low = lax.ppermute(last, axis, [(i, i + 1) for i in range(count - 1)])
    high = lax.ppermute(first, axis, [(i + 1, i) for i in range(count - 1)])
    return low, high


def body(proposal, flow_dual, shift_factors, outage_line, ratings, ramp_limit):
    limits = limits_of(outage_line, ratings)
    owned, periods = proposal.shape
    count = lax.axis_size("net")
    ring = count <= longest_ring and count % 2 == 0
    height = owned // chunks
    if ring:
        order = ring_order(count)
        ahead = by_distance(count)
        near = count - 3 if count > 4 else count // 2
        mine = jnp.array([order.index(i) for i in range(count)], jnp.int32)[lax.axis_index("net")]
        at = jnp.array(order, jnp.int32)[(mine + jnp.array(ahead, jnp.int32)) % count]
        factors = reorder(shift_factors, at)
        cut = near * owned

    def forward(pieces):
        pieces = [p.astype(jnp.bfloat16) for p in pieces]
        if not ring:
            whole = lax.all_gather(jnp.concatenate(pieces, axis=0), "net", axis=0, tiled=True)
            return jnp.dot(shift_factors, whole, preferred_element_type=jnp.float32)
        got = ring_gather(pieces, order)
        flows = 0.0
        for group, cols in ((ahead[:near], slice(0, cut)), (ahead[near:], slice(cut, None))):
            blocks = jnp.concatenate([got[c][d] for d in group for c in range(chunks)], axis=0)
            flows = flows + jnp.dot(factors[:, cols], blocks, preferred_element_type=jnp.float32)
        return flows

    def backward(misfit):
        narrow = misfit.astype(jnp.bfloat16)

        def share(cols):
            return lax.dot_general(cols, narrow, (((0,), (0,)), ((), ())), preferred_element_type=jnp.float32)

        if not ring:
            spread = lax.psum_scatter(share(shift_factors), "net", scatter_dimension=0, tiled=True)
            return [spread[c * height : (c + 1) * height] for c in range(chunks)]
        part = [{} for _ in range(chunks)]
        for group, cols in ((ahead[near:], slice(cut, None)), (ahead[:near], slice(0, cut))):
            spread = share(factors[:, cols])
            for j, d in enumerate(group):
                for c in range(chunks):
                    low = j * owned + c * height
                    part[c][d] = spread[low : low + height]
        return ring_scatter(part, order)

    pieces = [proposal[c * height : (c + 1) * height] for c in range(chunks)]
    dual = flow_dual
    sums = []
    for _ in range(passes):
        misfit, dual = project(forward(pieces), dual, limits)
        sums.append(jnp.sum(misfit * misfit))
        pieces = [p - relax_step * s for p, s in zip(pieces, backward(misfit))]
    inject = jnp.concatenate(pieces, axis=0)
    sums = total_over(total_over(jnp.stack(sums), "tm"), "net")
    entries = jnp.float32(shift_factors.shape[0] * count * periods * lax.axis_size("tm"))
    residual_norms = jnp.sqrt(sums / entries)
    low, high = beside(inject, "tm")
    padded = jnp.concatenate([low, inject, high], axis=1)
    step = padded[:, 1:] - padded[:, :-1]
    bound = ramp_limit[:, None]
    moment = lax.axis_index("tm") * periods + lax.broadcasted_iota(jnp.int32, (1, periods + 1), 1)
    valid = (moment >= 1) & (moment <= periods * lax.axis_size("tm") - 1)
    excess = jnp.where(valid, step - jnp.clip(step, -bound, bound), 0.0)
    dispatch = inject - 0.5 * excess[:, :-1] + 0.5 * excess[:, 1:]
    return (dispatch, dual, residual_norms)


def solution(mesh):
    return jax.shard_map(
        body,
        mesh=mesh,
        in_specs=(
            P(("groups", "net"), "tm"),
            P(("groups", "net"), "tm"),
            P("net", None),
            P("net"),
            P(),
            P("net"),
        ),
        out_specs=(P(("groups", "net"), "tm"), P(("groups", "net"), "tm"), P("groups")),
        check_vma=False,
    )
```

```python
import functools

import jax
import jax.numpy as jnp
from jax import lax
from jax.experimental import pallas as pl
from jax.experimental.pallas import tpu as pltpu
from jax.sharding import PartitionSpec as P

relax_step = 0.1
chunks = 2
passes = 2
longest_ring = 8


def ring_order(count):
    return list(range(0, count, 2)) + list(range(count - 1 - count % 2, 0, -2))


def hop_counts(count, chunk):
    far, near = count // 2, (count - 1) // 2
    return (near, far) if chunk % 2 else (far, near)


def gather_sends(count):
    sends = []
    for hop in range(1, count // 2 + 1):
        for flip in (0, 1):
            for chunk in range(chunks):
                for way in (1, -1):
                    limit = hop_counts(count, chunk)[0 if way == 1 else 1]
                    if hop <= limit and (chunk % 2 == (way == -1)) == (flip == 0):
                        sends.append((chunk, way, hop))
    return sends


def scatter_sends(count):
    return gather_sends(count)[::-1]


def hop_to(block, send, order):
    count = len(order)
    pairs = [(order[i], order[(i + send[1]) % count]) for i in range(count)]
    return lax.ppermute(block, "net", pairs)


def by_distance(count):
    out = [0]
    for hop in range(1, count // 2 + 1):
        out += [count - hop] if 2 * hop == count else [count - hop, hop]
    return out


def ring_gather(pieces, order):
    count = len(order)
    got = [{0: p} for p in pieces]
    held = {}
    for send in gather_sends(count):
        chunk, way, hop = send
        block = hop_to(held.get((chunk, way), pieces[chunk]), send, order)
        held[chunk, way] = block
        got[chunk][(-way * hop) % count] = block
    return got


def whole_in_vmem(count):
    return [pl.BlockSpec(memory_space=pltpu.VMEM)] * count


def small_call(kernel, out_shape, *operands):
    touched = sum(x.size * x.dtype.itemsize for x in jax.tree.leaves(out_shape)) * 3
    return pl.pallas_call(
        kernel,
        out_shape=out_shape,
        in_specs=whole_in_vmem(len(operands)),
        out_specs=jax.tree.map(lambda _: pl.BlockSpec(memory_space=pltpu.VMEM), out_shape),
        compiler_params=pltpu.CompilerParams(vmem_limit_bytes=16 << 20),
        cost_estimate=pl.CostEstimate(flops=0, transcendentals=0, bytes_accessed=touched),
    )(*operands)


def sum_kernel(low, spread_ref, arrived_ref, out_ref):
    mine = spread_ref[pl.ds(low, out_ref.shape[0]), :]
    out_ref[...] = (mine + arrived_ref[...].astype(jnp.float32)).astype(out_ref.dtype)


def update_kernel(low, spread_ref, ahead_ref, behind_ref, inject_ref, *out_refs):
    total = spread_ref[pl.ds(low, inject_ref.shape[0]), :]
    total = total + ahead_ref[...].astype(jnp.float32) + behind_ref[...].astype(jnp.float32)
    inject = inject_ref[...] - relax_step * total
    for ref in out_refs:
        ref[...] = inject.astype(ref.dtype)


def ring_scatter(part, order, height):
    count = len(order)
    held = {}
    for send in scatter_sends(count):
        chunk, way, hop = send
        spread, low = part(chunk, (way * hop) % count)
        if (chunk, way) in held:
            arrived = held[chunk, way]
            shape = jax.ShapeDtypeStruct(arrived.shape, arrived.dtype)
            mine = small_call(functools.partial(sum_kernel, low), shape, spread, arrived)
        else:
            mine = spread[low : low + height].astype(jnp.bfloat16)
        held[chunk, way] = hop_to(mine, send, order)
    return held


def place_of(position, count):
    return jnp.where(position % 2 == 0, position // 2, count - 1 - position // 2)


def at_place(place, count):
    return jnp.where(place < count // 2, 2 * place, 2 * (count - place) - 1)


def reorder_kernel(ahead, here_ref, factors_ref, out_ref, sems):
    count = len(ahead)
    width = out_ref.shape[1] // count
    mine = place_of(here_ref[0], count)
    copies = []
    for j, distance in enumerate(ahead):
        source = at_place((mine + distance) % count, count) * width
        copies.append(
            pltpu.make_async_copy(
                factors_ref.at[:, pl.ds(pl.multiple_of(source, width), width)],
                out_ref.at[:, pl.ds(j * width, width)],
                sems.at[j],
            )
        )
    for copy in copies:
        copy.start()
    for copy in copies:
        copy.wait()


def reorder(factors, ahead):
    return pl.pallas_call(
        functools.partial(reorder_kernel, tuple(ahead)),
        out_shape=jax.ShapeDtypeStruct(factors.shape, factors.dtype),
        in_specs=[pl.BlockSpec(memory_space=pltpu.SMEM), pl.BlockSpec(memory_space=pltpu.HBM)],
        out_specs=pl.BlockSpec(memory_space=pltpu.VMEM),
        scratch_shapes=[pltpu.SemaphoreType.DMA((len(ahead),))],
        compiler_params=pltpu.CompilerParams(vmem_limit_bytes=20 << 20),
        cost_estimate=pl.CostEstimate(flops=0, transcendentals=0, bytes_accessed=factors.size * factors.dtype.itemsize),
    )(lax.axis_index("net").reshape(1), factors)


def limits_of(outage_line, ratings):
    levels = lax.broadcasted_iota(jnp.int32, (outage_line.shape[0], ratings.shape[0]), 1)
    return jnp.sum(jnp.where(outage_line[:, None] == levels, ratings[None, :], 0.0), axis=1)


def project(flows, dual, limits):
    bound = limits[:, None]
    kept = jnp.clip(flows + dual, -bound, bound)
    misfit = flows - kept
    return (misfit, dual + misfit)


def exchanges(axes):
    out = []
    for axis, count in axes:
        if count & (count - 1):
            return None
        out += [(axis, 1 << k) for k in range(count.bit_length() - 1)]
    return out


def total_over(value, axes):
    steps = exchanges([(axis, lax.axis_size(axis)) for axis in axes])
    if steps is None:
        return lax.psum(value, axes)
    for axis, bit in steps:
        value = value + lax.ppermute(value, axis, [(i, i ^ bit) for i in range(lax.axis_size(axis))])
    return value


def beside(block, axis):
    count = lax.axis_size(axis)
    first, last = block[:, :1], block[:, -1:]
    zeros = jnp.zeros_like(first)
    if count == 1:
        return zeros, zeros
    if count == 2:
        at = lax.axis_index(axis)
        other = lax.ppermute(jnp.where(at == 0, last, first), axis, [(0, 1), (1, 0)])
        return jnp.where(at == 0, zeros, other), jnp.where(at == 0, other, zeros)
    low = lax.ppermute(last, axis, [(i, i + 1) for i in range(count - 1)])
    high = lax.ppermute(first, axis, [(i + 1, i) for i in range(count - 1)])
    return low, high


def body(proposal, flow_dual, shift_factors, outage_line, ratings, ramp_limit):
    limits = limits_of(outage_line, ratings)
    owned, periods = proposal.shape
    count = lax.axis_size("net")
    ring = count <= longest_ring and count % 2 == 0
    height = owned // chunks
    if ring:
        order = ring_order(count)
        ahead = by_distance(count)
        near = count - 3 if count > 4 else count // 2
        factors = reorder(shift_factors, ahead)
        cut = near * owned

    def forward(pieces):
        if not ring:
            whole = lax.all_gather(jnp.concatenate(pieces, axis=0), "net", axis=0, tiled=True)
            return jnp.dot(shift_factors, whole, preferred_element_type=jnp.float32)
        got = ring_gather(pieces, order)
        flows = 0.0
        for group, cols in ((ahead[:near], slice(0, cut)), (ahead[near:], slice(cut, None))):
            blocks = jnp.concatenate([got[c][d] for d in group for c in range(chunks)], axis=0)
            flows = flows + jnp.dot(factors[:, cols], blocks, preferred_element_type=jnp.float32)
        return flows

    def backward(stage, misfit, pieces):
        narrow = misfit.astype(jnp.bfloat16)

        def share(cols):
            return lax.dot_general(cols, narrow, (((0,), (0,)), ((), ())), preferred_element_type=jnp.float32)

        if not ring:
            spread = lax.psum_scatter(share(shift_factors), "net", scatter_dimension=0, tiled=True)
            pieces = [p - relax_step * spread[c * height : (c + 1) * height] for c, p in enumerate(pieces)]
            return pieces, [p.astype(jnp.bfloat16) for p in pieces]
        far, close = share(factors[:, cut:]), share(factors[:, :cut])

        def part(chunk, distance):
            j = ahead.index(distance)
            spread, first = (close, 0) if j < near else (far, near)
            return spread, (j - first) * owned + chunk * height

        held = ring_scatter(part, order, height)
        wide, slim = [], []
        for c, p in enumerate(pieces):
            shapes = [jax.ShapeDtypeStruct(p.shape, jnp.float32)]
            if stage + 1 < passes:
                shapes.append(jax.ShapeDtypeStruct(p.shape, jnp.bfloat16))
            spread, low = part(c, 0)
            new = small_call(functools.partial(update_kernel, low), shapes, spread, held[c, 1], held[c, -1], p)
            wide.append(new[0])
            slim.append(new[-1])
        return wide, slim

    pieces = [proposal[c * height : (c + 1) * height] for c in range(chunks)]
    slim = [p.astype(jnp.bfloat16) for p in pieces]
    dual = flow_dual
    sums = []
    for stage in range(passes):
        misfit, dual = project(forward(slim), dual, limits)
        sums.append(jnp.sum((misfit * misfit).reshape(-1, 8, periods), axis=0))
        pieces, slim = backward(stage, misfit, pieces)
    inject = jnp.concatenate(pieces, axis=0)
    sums = total_over(jnp.concatenate(sums, axis=0), ("tm", "net"))
    sums = jnp.sum(sums.reshape(passes, -1), axis=1)
    entries = jnp.float32(shift_factors.shape[0] * count * periods * lax.axis_size("tm"))
    residual_norms = jnp.sqrt(sums / entries)
    low, high = beside(inject, "tm")
    padded = jnp.concatenate([low, inject, high], axis=1)
    step = padded[:, 1:] - padded[:, :-1]
    bound = ramp_limit[:, None]
    moment = lax.axis_index("tm") * periods + lax.broadcasted_iota(jnp.int32, (1, periods + 1), 1)
    valid = (moment >= 1) & (moment <= periods * lax.axis_size("tm") - 1)
    excess = jnp.where(valid, step - jnp.clip(step, -bound, bound), 0.0)
    dispatch = inject - 0.5 * excess[:, :-1] + 0.5 * excess[:, 1:]
    return (dispatch, dual, residual_norms)


def solution(mesh):
    return jax.shard_map(
        body,
        mesh=mesh,
        in_specs=(
            P(("groups", "net"), "tm"),
            P(("groups", "net"), "tm"),
            P("net", None),
            P("net"),
            P(),
            P("net"),
        ),
        out_specs=(P(("groups", "net"), "tm"), P(("groups", "net"), "tm"), P("groups")),
        check_vma=False,
    )
```

```python
import functools

import jax
import jax.numpy as jnp
from jax import lax
from jax.experimental import pallas as pl
from jax.experimental.pallas import tpu as pltpu
from jax.sharding import PartitionSpec as P

relax_step = 0.1
chunks = 2
passes = 2
longest_ring = 8


def is_ring(count, split):
    return 4 <= count <= longest_ring and count % 2 == 0 and split == 2


def ring_order(count):
    return list(range(0, count, 2)) + list(range(count - 1 - count % 2, 0, -2))


def hop_counts(count, chunk):
    far, near = count // 2, (count - 1) // 2
    return (near, far) if chunk % 2 else (far, near)


def gather_sends(count):
    sends = []
    for hop in range(1, count // 2 + 1):
        for flip in (0, 1):
            for chunk in range(chunks):
                for way in (1, -1):
                    limit = hop_counts(count, chunk)[0 if way == 1 else 1]
                    if hop <= limit and (chunk % 2 == (way == -1)) == (flip == 0):
                        sends.append((chunk, way, hop))
    return sends


def scatter_sends(count):
    return gather_sends(count)[::-1]


def hop_to(block, send, order):
    count = len(order)
    pairs = [(order[i], order[(i + send[1]) % count]) for i in range(count)]
    return lax.ppermute(block, "net", pairs)


def by_distance(count):
    out = [0]
    for hop in range(1, count // 2 + 1):
        out += [count - hop] if 2 * hop == count else [count - hop, hop]
    return out


def ring_groups(count):
    order = by_distance(count)
    cuts = sorted({0, min(3, count), max(count - 3, min(3, count)), count - 1, count})
    return [order[a:b] for a, b in zip(cuts, cuts[1:])]


def ring_gather(pieces, order):
    count = len(order)
    got = [{0: p} for p in pieces]
    held = {}
    for send in gather_sends(count):
        chunk, way, hop = send
        block = hop_to(held.get((chunk, way), pieces[chunk]), send, order)
        held[chunk, way] = block
        got[chunk][(-way * hop) % count] = block
    return got


def small_call(kernel, out_shape, *operands):
    touched = sum(x.size * x.dtype.itemsize for x in jax.tree.leaves(out_shape)) * 3
    return pl.pallas_call(
        kernel,
        out_shape=out_shape,
        in_specs=[pl.BlockSpec(memory_space=pltpu.SMEM if x.dtype == jnp.int32 else pltpu.VMEM) for x in operands],
        out_specs=jax.tree.map(lambda _: pl.BlockSpec(memory_space=pltpu.VMEM), out_shape),
        compiler_params=pltpu.CompilerParams(vmem_limit_bytes=16 << 20),
        cost_estimate=pl.CostEstimate(flops=0, transcendentals=0, bytes_accessed=touched),
    )(*operands)


def sum_kernel(low, spread_ref, arrived_ref, out_ref):
    mine = spread_ref[pl.ds(low, out_ref.shape[0]), :]
    out_ref[...] = (mine + arrived_ref[...].astype(jnp.float32)).astype(out_ref.dtype)


def update_kernel(lows, spread_ref, *refs):
    ahead, behind, inject_ref, out_ref, slim = refs[:chunks], refs[chunks : 2 * chunks], refs[2 * chunks], refs[2 * chunks + 1], refs[2 * chunks + 2 :]
    height = ahead[0].shape[0]
    for c, low in enumerate(lows):
        rows = pl.ds(c * height, height)
        total = spread_ref[pl.ds(low, height), :]
        total = total + ahead[c][...].astype(jnp.float32) + behind[c][...].astype(jnp.float32)
        inject = inject_ref[rows, :] - relax_step * total
        out_ref[rows, :] = inject
        slim[c][...] = inject.astype(slim[c].dtype)


def ring_scatter(part, order, height):
    count = len(order)
    held = {}
    for send in scatter_sends(count):
        chunk, way, hop = send
        spread, low = part(chunk, (way * hop) % count)
        if (chunk, way) in held:
            arrived = held[chunk, way]
            shape = jax.ShapeDtypeStruct(arrived.shape, arrived.dtype)
            mine = small_call(functools.partial(sum_kernel, low), shape, spread, arrived)
        else:
            mine = spread[low : low + height].astype(jnp.bfloat16)
        held[chunk, way] = hop_to(mine, send, order)
    return held


def place_of(position, count):
    return jnp.where(position % 2 == 0, position // 2, count - 1 - position // 2)


def at_place(place, count):
    return jnp.where(place < count // 2, 2 * place, 2 * (count - place) - 1)


def reorder_kernel(distances, count, here_ref, factors_ref, out_ref, sems):
    width = factors_ref.shape[1] // count
    mine = place_of(here_ref[0], count)
    copies = []
    for j, distance in enumerate(distances):
        source = at_place((mine + distance) % count, count) * width
        copies.append(
            pltpu.make_async_copy(
                factors_ref.at[:, pl.ds(pl.multiple_of(source, width), width)],
                out_ref.at[:, pl.ds(j * width, width)],
                sems.at[j],
            )
        )
    for copy in copies:
        copy.start()
    for copy in copies:
        copy.wait()


def reorder(here, factors, distances, count):
    rows, width = factors.shape[0], factors.shape[1] // count * len(distances)
    return pl.pallas_call(
        functools.partial(reorder_kernel, tuple(distances), count),
        out_shape=jax.ShapeDtypeStruct((rows, width), factors.dtype),
        in_specs=[pl.BlockSpec(memory_space=pltpu.SMEM), pl.BlockSpec(memory_space=pltpu.HBM)],
        out_specs=pl.BlockSpec(memory_space=pltpu.VMEM),
        scratch_shapes=[pltpu.SemaphoreType.DMA((len(distances),))],
        compiler_params=pltpu.CompilerParams(vmem_limit_bytes=50 << 20),
        cost_estimate=pl.CostEstimate(flops=0, transcendentals=0, bytes_accessed=rows * width * factors.dtype.itemsize),
    )(here, factors)


def narrow_kernel(wide_ref, *out_refs):
    height = out_refs[0].shape[0]
    for c, ref in enumerate(out_refs):
        ref[...] = wide_ref[pl.ds(c * height, height), :].astype(ref.dtype)


def last_update_kernel(lows, here_ref, *refs):
    spread_ref, ahead, behind = refs[0], refs[1 : chunks + 1], refs[chunks + 1 : 2 * chunks + 1]
    inject_ref, out_ref, edge_ref = refs[2 * chunks + 1 :]
    height = ahead[0].shape[0]
    first = here_ref[1] == 0
    for c, low in enumerate(lows):
        rows = pl.ds(c * height, height)
        total = spread_ref[pl.ds(low, height), :]
        total = total + ahead[c][...].astype(jnp.float32) + behind[c][...].astype(jnp.float32)
        inject = inject_ref[rows, :] - relax_step * total
        out_ref[rows, :] = inject
        edge_ref[rows, :] = jnp.where(first, inject[:, -1:], inject[:, :1])


def ramp_kernel(here_ref, inject_ref, edge_ref, bound_ref, out_ref):
    first = here_ref[1] == 0
    inject, edge, bound = inject_ref[...], edge_ref[...], bound_ref[...]
    periods = inject.shape[1]
    lane = lax.broadcasted_iota(jnp.int32, inject.shape, 1)

    def excess(step):
        return step - jnp.clip(step, -bound, bound)

    before = jnp.where(lane == 0, edge, pltpu.roll(inject, 1, 1))
    after = jnp.where(lane == periods - 1, edge, pltpu.roll(inject, periods - 1, 1))
    low = jnp.where((lane == 0) & first, 0.0, excess(inject - before))
    high = jnp.where((lane == periods - 1) & jnp.logical_not(first), 0.0, excess(after - inject))
    out_ref[...] = inject - 0.5 * low + 0.5 * high


def norms_kernel(entries, sums_ref, out_ref):
    lane = lax.broadcasted_iota(jnp.int32, out_ref.shape, 1)
    out = jnp.zeros(out_ref.shape, jnp.float32)
    for k in range(passes):
        out = jnp.where(lane == k, jnp.sum(sums_ref[pl.ds(8 * k, 8), :]), out)
    out_ref[...] = jnp.sqrt(out / entries)


def limits_of(outage_line, ratings):
    levels = lax.broadcasted_iota(jnp.int32, (outage_line.shape[0], ratings.shape[0]), 1)
    return jnp.sum(jnp.where(outage_line[:, None] == levels, ratings[None, :], 0.0), axis=1)


def project(flows, dual, limits):
    bound = limits[:, None]
    kept = jnp.clip(flows + dual, -bound, bound)
    misfit = flows - kept
    return (misfit, dual + misfit)


def exchanges(axes):
    out = []
    for axis, count in axes:
        if count & (count - 1):
            return None
        out += [(axis, 1 << k) for k in range(count.bit_length() - 1)]
    return out


def total_over(value, axes):
    steps = exchanges([(axis, lax.axis_size(axis)) for axis in axes])
    if steps is None:
        return lax.psum(value, axes)
    for axis, bit in steps:
        value = value + lax.ppermute(value, axis, [(i, i ^ bit) for i in range(lax.axis_size(axis))])
    return value


def beside(block, axis):
    count = lax.axis_size(axis)
    first, last = block[:, :1], block[:, -1:]
    zeros = jnp.zeros_like(first)
    if count == 1:
        return zeros, zeros
    if count == 2:
        at = lax.axis_index(axis)
        other = lax.ppermute(jnp.where(at == 0, last, first), axis, [(0, 1), (1, 0)])
        return jnp.where(at == 0, zeros, other), jnp.where(at == 0, other, zeros)
    low = lax.ppermute(last, axis, [(i, i + 1) for i in range(count - 1)])
    high = lax.ppermute(first, axis, [(i + 1, i) for i in range(count - 1)])
    return low, high


def body(proposal, flow_dual, shift_factors, outage_line, ratings, ramp_limit):
    limits = limits_of(outage_line, ratings)
    owned, periods = proposal.shape
    count = lax.axis_size("net")
    ring = is_ring(count, lax.axis_size("tm"))
    height = owned // chunks
    here = jnp.stack([lax.axis_index("net"), lax.axis_index("tm")]).astype(jnp.int32)
    if ring:
        order = ring_order(count)
        groups = ring_groups(count)
        factors = []
        for group in groups:
            factors.append(reorder(here, shift_factors, group, count))

    def forward(pieces):
        if not ring:
            whole = lax.all_gather(jnp.concatenate(pieces, axis=0), "net", axis=0, tiled=True)
            return jnp.dot(shift_factors, whole, preferred_element_type=jnp.float32)
        got = ring_gather(pieces, order)
        flows = None
        for group, cols in zip(groups, factors):
            blocks = jnp.concatenate([got[c][d] for d in group for c in range(chunks)], axis=0)
            share = jnp.dot(cols, blocks, preferred_element_type=jnp.float32)
            flows = share if flows is None else flows + share
        return flows

    def backward(misfit):
        narrow = misfit.astype(jnp.bfloat16)
        shares = {}
        for group, cols in reversed(list(zip(groups, factors))):
            spread = lax.dot_general(cols, narrow, (((0,), (0,)), ((), ())), preferred_element_type=jnp.float32)
            for j, d in enumerate(group):
                for c in range(chunks):
                    shares[c, d] = (spread, j * owned + c * height)
        held = ring_scatter(lambda c, d: shares[c, d], order, height)
        return [shares[c, 0] for c in range(chunks)], held

    dual = flow_dual
    sums = []
    entries = float(shift_factors.shape[0] * count * periods * lax.axis_size("tm"))
    if not ring:
        inject = proposal
        for _ in range(passes):
            misfit, dual = project(forward([inject.astype(jnp.bfloat16)]), dual, limits)
            sums.append(jnp.sum(misfit * misfit))
            share = lax.dot_general(
                shift_factors,
                misfit.astype(jnp.bfloat16),
                (((0,), (0,)), ((), ())),
                preferred_element_type=jnp.float32,
            )
            inject = inject - relax_step * lax.psum_scatter(share, "net", scatter_dimension=0, tiled=True)
        norms = jnp.sqrt(total_over(jnp.stack(sums), ("tm", "net")) / entries)
        return (ramp(inject, ramp_limit), dual, norms)

    chunk_shape = jax.ShapeDtypeStruct((height, periods), jnp.bfloat16)
    whole_shape = jax.ShapeDtypeStruct((owned, periods), jnp.float32)
    slim = small_call(narrow_kernel, [chunk_shape] * chunks, proposal)
    bound = jnp.broadcast_to(ramp_limit[:, None], (owned, periods))
    inject = proposal
    for stage in range(passes):
        misfit, dual = project(forward(slim), dual, limits)
        sums.append(jnp.sum((misfit * misfit).reshape(-1, 8, periods), axis=0))
        own, held = backward(misfit)
        lows = tuple(low for _, low in own)
        arrived = [held[c, way] for way in (1, -1) for c in range(chunks)]
        if stage + 1 < passes:
            inject, *slim = small_call(
                functools.partial(update_kernel, lows),
                [whole_shape] + [chunk_shape] * chunks,
                own[0][0],
                *arrived,
                inject,
            )
        else:
            inject, edge = small_call(
                functools.partial(last_update_kernel, lows),
                [whole_shape, jax.ShapeDtypeStruct((owned, 1), jnp.float32)],
                here,
                own[0][0],
                *arrived,
                inject,
            )
    sums = total_over(jnp.concatenate(sums, axis=0), ("tm", "net"))
    tile = jax.ShapeDtypeStruct((8, periods), jnp.float32)
    norms = small_call(functools.partial(norms_kernel, entries), tile, sums)[0, :passes]
    edge = lax.ppermute(edge, "tm", [(0, 1), (1, 0)])
    dispatch = small_call(ramp_kernel, whole_shape, here, inject, edge, bound)
    return (dispatch, dual, norms)


def ramp(inject, ramp_limit):
    periods = inject.shape[1]
    low, high = beside(inject, "tm")
    padded = jnp.concatenate([low, inject, high], axis=1)
    step = padded[:, 1:] - padded[:, :-1]
    bound = ramp_limit[:, None]
    moment = lax.axis_index("tm") * periods + lax.broadcasted_iota(jnp.int32, (1, periods + 1), 1)
    valid = (moment >= 1) & (moment <= periods * lax.axis_size("tm") - 1)
    excess = jnp.where(valid, step - jnp.clip(step, -bound, bound), 0.0)
    return inject - 0.5 * excess[:, :-1] + 0.5 * excess[:, 1:]


def solution(mesh):
    return jax.shard_map(
        body,
        mesh=mesh,
        in_specs=(
            P(("groups", "net"), "tm"),
            P(("groups", "net"), "tm"),
            P("net", None),
            P("net"),
            P(),
            P("net"),
        ),
        out_specs=(P(("groups", "net"), "tm"), P(("groups", "net"), "tm"), P("groups")),
        check_vma=False,
    )
```

```python
import functools

import jax
import jax.numpy as jnp
from jax import lax
from jax.experimental import pallas as pl
from jax.experimental.pallas import tpu as pltpu
from jax.sharding import PartitionSpec as P

relax_step = 0.1
chunks = 2
passes = 2
longest_ring = 8


def is_ring(count, split):
    return 4 <= count <= longest_ring and count % 2 == 0 and split == 2


def ring_order(count):
    return list(range(0, count, 2)) + list(range(count - 1 - count % 2, 0, -2))


def hop_counts(count, chunk):
    far, near = count // 2, (count - 1) // 2
    return (near, far) if chunk % 2 else (far, near)


def gather_sends(count):
    sends = []
    for hop in range(1, count // 2 + 1):
        for flip in (0, 1):
            for chunk in range(chunks):
                for way in (1, -1):
                    limit = hop_counts(count, chunk)[0 if way == 1 else 1]
                    if hop <= limit and (chunk % 2 == (way == -1)) == (flip == 0):
                        sends.append((chunk, way, hop))
    return sends


def scatter_sends(count):
    return gather_sends(count)[::-1]


def hop_to(block, send, order):
    count = len(order)
    pairs = [(order[i], order[(i + send[1]) % count]) for i in range(count)]
    return lax.ppermute(block, "net", pairs)


def by_distance(count):
    out = [0]
    for hop in range(1, count // 2 + 1):
        out += [count - hop] if 2 * hop == count else [count - hop, hop]
    return out


def ring_groups(count):
    order = by_distance(count)
    cuts = sorted({0, min(3, count), max(count - 3, min(3, count)), count - 1, count})
    return [order[a:b] for a, b in zip(cuts, cuts[1:])]


def reorder_parts(groups):
    return [[g] for g in groups[:-2]] + [groups[-2:]]


def ring_gather(pieces, order):
    count = len(order)
    got = [{0: p} for p in pieces]
    held = {}
    for send in gather_sends(count):
        chunk, way, hop = send
        block = hop_to(held.get((chunk, way), pieces[chunk]), send, order)
        held[chunk, way] = block
        got[chunk][(-way * hop) % count] = block
    return got


def small_call(kernel, out_shape, *operands):
    touched = sum(x.size * x.dtype.itemsize for x in jax.tree.leaves(out_shape)) * 3
    return pl.pallas_call(
        kernel,
        out_shape=out_shape,
        in_specs=[pl.BlockSpec(memory_space=pltpu.SMEM if x.dtype == jnp.int32 else pltpu.VMEM) for x in operands],
        out_specs=jax.tree.map(lambda x: pl.BlockSpec(memory_space=pltpu.VMEM if x.ndim > 1 else pltpu.SMEM), out_shape),
        compiler_params=pltpu.CompilerParams(vmem_limit_bytes=16 << 20),
        cost_estimate=pl.CostEstimate(flops=0, transcendentals=0, bytes_accessed=touched),
    )(*operands)


def first_kernel(low, height, spread_ref, *refs):
    out_ref = refs[-1]
    out_ref[pl.ds(0, height), :] = spread_ref[pl.ds(low, height), :].astype(out_ref.dtype)
    if len(refs) > 1:
        out_ref[pl.ds(height, refs[0].shape[0]), :] = refs[0][...]


def add_kernel(left_ref, right_ref, out_ref):
    out_ref[...] = left_ref[...] + right_ref[...]


def sum_kernel(low, height, spread_ref, arrived_ref, out_ref):
    mine = spread_ref[pl.ds(low, height), :]
    top, rest = pl.ds(0, height), out_ref.shape[0] - height
    out_ref[top, :] = (mine + arrived_ref[top, :].astype(jnp.float32)).astype(out_ref.dtype)
    if rest:
        out_ref[pl.ds(height, rest), :] = arrived_ref[pl.ds(height, rest), :]


def update_kernel(lows, spread_ref, *refs):
    ahead, behind, inject_ref, out_ref, slim = refs[:chunks], refs[chunks : 2 * chunks], refs[2 * chunks], refs[2 * chunks + 1], refs[2 * chunks + 2 :]
    height = ahead[0].shape[0]
    for c, low in enumerate(lows):
        rows = pl.ds(c * height, height)
        total = spread_ref[pl.ds(low, height), :]
        total = total + ahead[c][...].astype(jnp.float32) + behind[c][...].astype(jnp.float32)
        inject = inject_ref[rows, :] - relax_step * total
        out_ref[rows, :] = inject
        slim[c][...] = inject.astype(slim[c].dtype)


def ring_scatter(part, order, height, extra=None):
    count = len(order)
    held, tiles = {}, []
    for send in scatter_sends(count):
        chunk, way, hop = send
        spread, low = part(chunk, (way * hop) % count)
        more = extra is not None and chunk == 0
        rows = height + (extra.shape[0] if more else 0)
        shape = jax.ShapeDtypeStruct((rows, spread.shape[1]), jnp.bfloat16)
        if (chunk, way) in held:
            kernel, tail = sum_kernel, [held[chunk, way]]
        else:
            kernel, tail = first_kernel, [extra] if more else []
        mine = small_call(functools.partial(kernel, low, height), shape, spread, *tail)
        held[chunk, way] = hop_to(mine, send, order)
        if more:
            tiles.append(held[chunk, way])
    return held, tiles


def place_of(position, count):
    return jnp.where(position % 2 == 0, position // 2, count - 1 - position // 2)


def at_place(place, count):
    return jnp.where(place < count // 2, 2 * place, 2 * (count - place) - 1)


def reorder_kernel(distances, count, here_ref, factors_ref, out_ref, sems):
    width = factors_ref.shape[1] // count
    mine = place_of(here_ref[0], count)
    copies = []
    for j, distance in enumerate(distances):
        source = at_place((mine + distance) % count, count) * width
        copies.append(
            pltpu.make_async_copy(
                factors_ref.at[:, pl.ds(pl.multiple_of(source, width), width)],
                out_ref.at[:, pl.ds(j * width, width)],
                sems.at[j],
            )
        )
    for copy in copies:
        copy.start()
    for copy in copies:
        copy.wait()


def reorder(here, factors, distances, count):
    rows, width = factors.shape[0], factors.shape[1] // count * len(distances)
    return pl.pallas_call(
        functools.partial(reorder_kernel, tuple(distances), count),
        out_shape=jax.ShapeDtypeStruct((rows, width), factors.dtype),
        in_specs=[pl.BlockSpec(memory_space=pltpu.SMEM), pl.BlockSpec(memory_space=pltpu.HBM)],
        out_specs=pl.BlockSpec(memory_space=pltpu.VMEM),
        scratch_shapes=[pltpu.SemaphoreType.DMA((len(distances),))],
        compiler_params=pltpu.CompilerParams(vmem_limit_bytes=50 << 20),
        cost_estimate=pl.CostEstimate(flops=0, transcendentals=0, bytes_accessed=rows * width * factors.dtype.itemsize),
    )(here, factors)


def narrow_kernel(wide_ref, *out_refs):
    height = out_refs[0].shape[0]
    for c, ref in enumerate(out_refs):
        ref[...] = wide_ref[pl.ds(c * height, height), :].astype(ref.dtype)


def last_update_kernel(lows, here_ref, *refs):
    spread_ref, ahead, behind = refs[0], refs[1 : chunks + 1], refs[chunks + 1 : 2 * chunks + 1]
    inject_ref, out_ref, edge_ref = refs[2 * chunks + 1 :]
    height, top = inject_ref.shape[0] // chunks, pl.ds(0, inject_ref.shape[0] // chunks)
    first = here_ref[1] == 0
    for c, low in enumerate(lows):
        rows = pl.ds(c * height, height)
        total = spread_ref[pl.ds(low, height), :]
        total = total + ahead[c][top, :].astype(jnp.float32) + behind[c][top, :].astype(jnp.float32)
        inject = inject_ref[rows, :] - relax_step * total
        out_ref[rows, :] = inject
        edge_ref[rows, :] = jnp.where(first, inject[:, -1:], inject[:, :1])


def excess_of(step, bound):
    return step - jnp.clip(step, -bound, bound)


def inner_ramp_kernel(inject_ref, bound_ref, out_ref):
    inject, bound = inject_ref[...], bound_ref[...]
    periods = inject.shape[1]
    lane = lax.broadcasted_iota(jnp.int32, inject.shape, 1)
    low = jnp.where(lane == 0, 0.0, excess_of(inject - pltpu.roll(inject, 1, 1), bound))
    high = jnp.where(lane == periods - 1, 0.0, pltpu.roll(low, periods - 1, 1))
    out_ref[...] = inject - 0.5 * low + 0.5 * high


def edge_ramp_kernel(here_ref, inner_ref, mine_ref, other_ref, bound_ref, out_ref, whole, sems):
    first = here_ref[1] == 0
    parts = sems.shape[0]
    rows, periods = whole.shape[0] // parts, whole.shape[1]
    edge = jnp.where(first, periods - 1, 0)
    copies = []
    for p in range(parts):
        at = pl.ds(p * rows, rows)
        mine, other, inner = mine_ref[at, :], other_ref[at, :], inner_ref[at, :]
        excess = excess_of(jnp.where(first, other - mine, mine - other), bound_ref[at, :1])
        share = jnp.where(first, 0.5 * excess, -0.5 * excess)
        lane = lax.broadcasted_iota(jnp.int32, inner.shape, 1)
        whole[at, :] = jnp.where(lane == edge, inner + share, inner)
        copy = pltpu.make_async_copy(whole.at[at, :], out_ref.at[at, :], sems.at[p])
        copy.start()
        copies.append(copy)
    for copy in copies:
        copy.wait()


def edge_ramp(here, inner, mine, other, bound):
    parts = 4
    return pl.pallas_call(
        edge_ramp_kernel,
        out_shape=jax.ShapeDtypeStruct(inner.shape, inner.dtype),
        in_specs=[pl.BlockSpec(memory_space=pltpu.SMEM)] + [pl.BlockSpec(memory_space=pltpu.VMEM)] * 4,
        out_specs=pl.BlockSpec(memory_space=pltpu.HBM),
        scratch_shapes=[pltpu.VMEM(inner.shape, inner.dtype), pltpu.SemaphoreType.DMA((parts,))],
        compiler_params=pltpu.CompilerParams(vmem_limit_bytes=16 << 20),
        cost_estimate=pl.CostEstimate(flops=0, transcendentals=0, bytes_accessed=2 * inner.size * inner.dtype.itemsize),
    )(here, inner, mine, other, bound)


def squares_kernel(misfit_ref, out_ref):
    misfit = misfit_ref[...]
    out_ref[...] = jnp.sum((misfit * misfit).reshape(-1, 8, misfit.shape[1]), axis=0)


def pack_kernel(*refs):
    *earlier, misfit_ref, out_ref = refs
    misfit = misfit_ref[...]
    sums = [ref[...] for ref in earlier] + [(misfit * misfit).reshape(-1, 8, misfit.shape[1])]
    row = lax.broadcasted_iota(jnp.int32, out_ref.shape, 0)
    out = jnp.zeros(out_ref.shape, jnp.float32)
    for k, value in enumerate(sums):
        left = jnp.sum(value.reshape(-1, misfit.shape[1]), axis=0, keepdims=True)
        for j in range(3):
            piece = left.astype(jnp.bfloat16).astype(jnp.float32)
            out = jnp.where(row == 3 * k + j, piece, out)
            left = left - piece
    out_ref[...] = out.astype(out_ref.dtype)


def unpack_kernel(own_ref, *refs):
    *tiles, out_ref = refs
    tall = own_ref.shape[0]
    total = own_ref[...].astype(jnp.float32)
    for ref in tiles:
        total = total + ref[pl.ds(ref.shape[0] - tall, tall), :].astype(jnp.float32)
    out_ref[...] = total


def norms_kernel(entries, left_ref, right_ref, out_ref):
    total = left_ref[...] + right_ref[...]
    row = lax.broadcasted_iota(jnp.int32, total.shape, 0)
    for k in range(passes):
        square = jnp.sum(jnp.where((row >= 3 * k) & (row < 3 * k + 3), total, 0.0), axis=0, keepdims=True)
        norm = jnp.sqrt(jnp.sum(square, axis=1, keepdims=True) / entries)
        out_ref[k] = jnp.sum(norm)


def limits_of(outage_line, ratings):
    levels = lax.broadcasted_iota(jnp.int32, (outage_line.shape[0], ratings.shape[0]), 1)
    return jnp.sum(jnp.where(outage_line[:, None] == levels, ratings[None, :], 0.0), axis=1)


def project(flows, dual, limits):
    bound = limits[:, None]
    kept = jnp.clip(flows + dual, -bound, bound)
    misfit = flows - kept
    return (misfit, dual + misfit)


def exchanges(axes):
    out = []
    for axis, count in axes:
        if count & (count - 1):
            return None
        out += [(axis, 1 << k) for k in range(count.bit_length() - 1)]
    return out


def total_over(value, axes):
    steps = exchanges([(axis, lax.axis_size(axis)) for axis in axes])
    if steps is None:
        return lax.psum(value, axes)
    for axis, bit in steps:
        value = value + lax.ppermute(value, axis, [(i, i ^ bit) for i in range(lax.axis_size(axis))])
    return value


def beside(block, axis):
    count = lax.axis_size(axis)
    first, last = block[:, :1], block[:, -1:]
    zeros = jnp.zeros_like(first)
    if count == 1:
        return zeros, zeros
    if count == 2:
        at = lax.axis_index(axis)
        other = lax.ppermute(jnp.where(at == 0, last, first), axis, [(0, 1), (1, 0)])
        return jnp.where(at == 0, zeros, other), jnp.where(at == 0, other, zeros)
    low = lax.ppermute(last, axis, [(i, i + 1) for i in range(count - 1)])
    high = lax.ppermute(first, axis, [(i + 1, i) for i in range(count - 1)])
    return low, high


def body(proposal, flow_dual, shift_factors, outage_line, ratings, ramp_limit):
    limits = limits_of(outage_line, ratings)
    owned, periods = proposal.shape
    count = lax.axis_size("net")
    ring = is_ring(count, lax.axis_size("tm"))
    height = owned // chunks
    here = jnp.stack([lax.axis_index("net"), lax.axis_index("tm")]).astype(jnp.int32)
    if ring:
        order = ring_order(count)
        groups = ring_groups(count)
        factors = []
        for part in reorder_parts(groups):
            side = reorder(here, shift_factors, [d for g in part for d in g], count)
            low = 0
            for g in part:
                factors.append(side[:, low : low + len(g) * owned])
                low += len(g) * owned

    def forward(pieces):
        if not ring:
            whole = lax.all_gather(jnp.concatenate(pieces, axis=0), "net", axis=0, tiled=True)
            return jnp.dot(shift_factors, whole, preferred_element_type=jnp.float32)
        got = ring_gather(pieces, order)
        flows = None
        for group, cols in zip(groups, factors):
            blocks = jnp.concatenate([got[c][d] for d in group for c in range(chunks)], axis=0)
            share = jnp.dot(cols, blocks, preferred_element_type=jnp.float32)
            flows = share if flows is None else flows + share
        return flows

    def backward(misfit, extra):
        narrow = misfit.astype(jnp.bfloat16)
        shares = {}
        for g in reversed(range(len(groups))):
            group, cols = groups[g], factors[g]
            spread = lax.dot_general(cols, narrow, (((0,), (0,)), ((), ())), preferred_element_type=jnp.float32)
            for j, d in enumerate(group):
                for c in range(chunks):
                    shares[c, d] = (spread, j * owned + c * height)
        held, tiles = ring_scatter(lambda c, d: shares[c, d], order, height, extra)
        return [shares[c, 0] for c in range(chunks)], held, tiles

    dual = flow_dual
    sums = []
    entries = float(shift_factors.shape[0] * count * periods * lax.axis_size("tm"))
    if not ring:
        inject = proposal
        for _ in range(passes):
            misfit, dual = project(forward([inject.astype(jnp.bfloat16)]), dual, limits)
            sums.append(jnp.sum(misfit * misfit))
            share = lax.dot_general(
                shift_factors,
                misfit.astype(jnp.bfloat16),
                (((0,), (0,)), ((), ())),
                preferred_element_type=jnp.float32,
            )
            inject = inject - relax_step * lax.psum_scatter(share, "net", scatter_dimension=0, tiled=True)
        norms = jnp.sqrt(total_over(jnp.stack(sums), ("tm", "net")) / entries)
        return (ramp(inject, ramp_limit), dual, norms)

    chunk_shape = jax.ShapeDtypeStruct((height, periods), jnp.bfloat16)
    whole_shape = jax.ShapeDtypeStruct((owned, periods), jnp.float32)
    slim = small_call(narrow_kernel, [chunk_shape] * chunks, proposal)
    bound = jnp.broadcast_to(ramp_limit[:, None], (owned, periods))
    inject = proposal
    for stage in range(passes):
        misfit, _ = project(forward(slim), dual, limits)
        dual = small_call(add_kernel, jax.ShapeDtypeStruct(dual.shape, dual.dtype), dual, misfit)
        if stage + 1 < passes:
            tile = jax.ShapeDtypeStruct((8, periods), jnp.float32)
            sums.append(small_call(squares_kernel, tile, misfit))
            extra = None
        else:
            tile = jax.ShapeDtypeStruct((16, periods), jnp.bfloat16)
            extra = small_call(pack_kernel, tile, *sums, misfit)
        own, held, tiles = backward(misfit, extra)
        lows = tuple(low for _, low in own)
        arrived = [held[c, way] for way in (1, -1) for c in range(chunks)]
        if stage + 1 < passes:
            inject, *slim = small_call(
                functools.partial(update_kernel, lows),
                [whole_shape] + [chunk_shape] * chunks,
                own[0][0],
                *arrived,
                inject,
            )
        else:
            inject, edge = small_call(
                functools.partial(last_update_kernel, lows),
                [whole_shape, jax.ShapeDtypeStruct((owned, 1), jnp.float32)],
                here,
                own[0][0],
                *arrived,
                inject,
            )
    other = lax.ppermute(edge, "tm", [(0, 1), (1, 0)])
    inner = small_call(inner_ramp_kernel, whole_shape, inject, bound)
    wide = jax.ShapeDtypeStruct(extra.shape, jnp.float32)
    sums = small_call(unpack_kernel, wide, extra, *tiles)
    others = lax.ppermute(sums, "tm", [(0, 1), (1, 0)])
    norms = small_call(
        functools.partial(norms_kernel, entries), jax.ShapeDtypeStruct((passes,), jnp.float32), sums, others
    )
    dispatch = edge_ramp(here, inner, edge, other, bound)
    return (dispatch, dual, norms)


def ramp(inject, ramp_limit):
    periods = inject.shape[1]
    low, high = beside(inject, "tm")
    padded = jnp.concatenate([low, inject, high], axis=1)
    step = padded[:, 1:] - padded[:, :-1]
    bound = ramp_limit[:, None]
    moment = lax.axis_index("tm") * periods + lax.broadcasted_iota(jnp.int32, (1, periods + 1), 1)
    valid = (moment >= 1) & (moment <= periods * lax.axis_size("tm") - 1)
    excess = jnp.where(valid, step - jnp.clip(step, -bound, bound), 0.0)
    return inject - 0.5 * excess[:, :-1] + 0.5 * excess[:, 1:]


def solution(mesh):
    return jax.shard_map(
        body,
        mesh=mesh,
        in_specs=(
            P(("groups", "net"), "tm"),
            P(("groups", "net"), "tm"),
            P("net", None),
            P("net"),
            P(),
            P("net"),
        ),
        out_specs=(P(("groups", "net"), "tm"), P(("groups", "net"), "tm"), P("groups")),
        check_vma=False,
    )
```

```python
import functools

import jax
import jax.numpy as jnp
from jax import lax
from jax.experimental import pallas as pl
from jax.experimental.pallas import tpu as pltpu
from jax.sharding import PartitionSpec as P

relax_step = 0.1
chunks = 2
passes = 2
longest_ring = 8


def is_ring(count, split):
    return 4 <= count <= longest_ring and count % 2 == 0 and split == 2


def ring_order(count):
    return list(range(0, count, 2)) + list(range(count - 1 - count % 2, 0, -2))


def hop_counts(count, chunk):
    far, near = count // 2, (count - 1) // 2
    return (near, far) if chunk % 2 else (far, near)


def gather_sends(count):
    sends = []
    for hop in range(1, count // 2 + 1):
        for flip in (0, 1):
            for chunk in range(chunks):
                for way in (1, -1):
                    limit = hop_counts(count, chunk)[0 if way == 1 else 1]
                    if hop <= limit and (chunk % 2 == (way == -1)) == (flip == 0):
                        sends.append((chunk, way, hop))
    return sends


def scatter_sends(count):
    return gather_sends(count)[::-1]


def hop_to(block, send, order):
    count = len(order)
    pairs = [(order[i], order[(i + send[1]) % count]) for i in range(count)]
    return lax.ppermute(block, "net", pairs)


def by_distance(count):
    out = [0]
    for hop in range(1, count // 2 + 1):
        out += [count - hop] if 2 * hop == count else [count - hop, hop]
    return out


def ring_groups(count):
    order = by_distance(count)
    cuts = sorted({0, min(3, count), max(count - 3, min(3, count)), count - 1, count})
    return [order[a:b] for a, b in zip(cuts, cuts[1:])]


def reorder_parts(groups):
    return [[g] for g in groups[:-2]] + [groups[-2:]]


def ring_gather(pieces, order):
    count = len(order)
    got = [{0: p} for p in pieces]
    held = {}
    for send in gather_sends(count):
        chunk, way, hop = send
        block = hop_to(held.get((chunk, way), pieces[chunk]), send, order)
        held[chunk, way] = block
        got[chunk][(-way * hop) % count] = block
    return got


def small_call(kernel, out_shape, *operands):
    touched = sum(x.size * x.dtype.itemsize for x in jax.tree.leaves(out_shape)) * 3
    return pl.pallas_call(
        kernel,
        out_shape=out_shape,
        in_specs=[pl.BlockSpec(memory_space=pltpu.VMEM)] * len(operands),
        out_specs=jax.tree.map(lambda x: pl.BlockSpec(memory_space=pltpu.VMEM if x.ndim > 1 else pltpu.SMEM), out_shape),
        compiler_params=pltpu.CompilerParams(vmem_limit_bytes=16 << 20),
        cost_estimate=pl.CostEstimate(flops=0, transcendentals=0, bytes_accessed=touched),
    )(*operands)


def first_kernel(low, height, spread_ref, *refs):
    out_ref = refs[-1]
    out_ref[pl.ds(0, height), :] = spread_ref[pl.ds(low, height), :].astype(out_ref.dtype)
    if len(refs) > 1:
        out_ref[pl.ds(height, refs[0].shape[0]), :] = refs[0][...]


def add_kernel(left_ref, right_ref, out_ref):
    out_ref[...] = left_ref[...] + right_ref[...]


def sum_kernel(low, height, spread_ref, arrived_ref, out_ref):
    mine = spread_ref[pl.ds(low, height), :]
    top, rest = pl.ds(0, height), out_ref.shape[0] - height
    out_ref[top, :] = (mine + arrived_ref[top, :].astype(jnp.float32)).astype(out_ref.dtype)
    if rest:
        out_ref[pl.ds(height, rest), :] = arrived_ref[pl.ds(height, rest), :]


def update_kernel(lows, spread_ref, *refs):
    ahead, behind, inject_ref, out_ref, slim = refs[:chunks], refs[chunks : 2 * chunks], refs[2 * chunks], refs[2 * chunks + 1], refs[2 * chunks + 2 :]
    height = ahead[0].shape[0]
    for c, low in enumerate(lows):
        rows = pl.ds(c * height, height)
        total = spread_ref[pl.ds(low, height), :]
        total = total + ahead[c][...].astype(jnp.float32) + behind[c][...].astype(jnp.float32)
        inject = inject_ref[rows, :] - relax_step * total
        out_ref[rows, :] = inject
        slim[c][...] = inject.astype(slim[c].dtype)


def ring_scatter(part, order, height, extra=None):
    count = len(order)
    held, tiles = {}, []
    for send in scatter_sends(count):
        chunk, way, hop = send
        spread, low = part(chunk, (way * hop) % count)
        more = extra is not None and chunk == chunks - 1
        rows = height + (extra.shape[0] if more else 0)
        shape = jax.ShapeDtypeStruct((rows, spread.shape[1]), jnp.bfloat16)
        if (chunk, way) in held:
            kernel, tail = sum_kernel, [held[chunk, way]]
        else:
            kernel, tail = first_kernel, [extra] if more else []
        mine = small_call(functools.partial(kernel, low, height), shape, spread, *tail)
        held[chunk, way] = hop_to(mine, send, order)
        if more:
            tiles.append(held[chunk, way])
    return held, tiles


def place_of(position, count):
    return jnp.where(position % 2 == 0, position // 2, count - 1 - position // 2)


def at_place(place, count):
    return jnp.where(place < count // 2, 2 * place, 2 * (count - place) - 1)


def reorder_kernel(distances, count, _, factors_ref, out_ref, sems):
    width = factors_ref.shape[1] // count
    mine = place_of(lax.axis_index("net"), count)
    copies = []
    for j, distance in enumerate(distances):
        source = at_place((mine + distance) % count, count) * width
        copies.append(
            pltpu.make_async_copy(
                factors_ref.at[:, pl.ds(pl.multiple_of(source, width), width)],
                out_ref.at[:, pl.ds(j * width, width)],
                sems.at[j],
            )
        )
    for copy in copies:
        copy.start()
    for copy in copies:
        copy.wait()


def reorder(factors, distances, count):
    rows, width = factors.shape[0], factors.shape[1] // count * len(distances)
    return pl.pallas_call(
        functools.partial(reorder_kernel, tuple(distances), count),
        out_shape=jax.ShapeDtypeStruct((rows, width), factors.dtype),
        in_specs=[pl.BlockSpec(memory_space=pl.ANY), pl.BlockSpec(memory_space=pltpu.HBM)],
        out_specs=pl.BlockSpec(memory_space=pltpu.VMEM),
        scratch_shapes=[pltpu.SemaphoreType.DMA((len(distances),))],
        compiler_params=pltpu.CompilerParams(vmem_limit_bytes=50 << 20),
        cost_estimate=pl.CostEstimate(flops=0, transcendentals=0, bytes_accessed=rows * width * factors.dtype.itemsize),
    )(lax.axis_index("net").reshape(1), factors)


def narrow_kernel(wide_ref, *out_refs):
    height = out_refs[0].shape[0]
    for c, ref in enumerate(out_refs):
        ref[...] = wide_ref[pl.ds(c * height, height), :].astype(ref.dtype)


def last_update_kernel(low, chunk, spread_ref, ahead_ref, behind_ref, inject_ref, out_ref):
    height = out_ref.shape[0]
    top = pl.ds(0, height)
    total = spread_ref[pl.ds(low, height), :]
    total = total + ahead_ref[top, :].astype(jnp.float32) + behind_ref[top, :].astype(jnp.float32)
    out_ref[...] = inject_ref[pl.ds(chunk * height, height), :] - relax_step * total


def excess_of(step, bound):
    return step - jnp.clip(step, -bound, bound)


def inner_ramp_kernel(*refs):
    *parts, bound_ref, out_ref = refs
    for c, ref in enumerate(parts):
        inject = ref[...]
        rows, periods = inject.shape
        at = pl.ds(c * rows, rows)
        lane = lax.broadcasted_iota(jnp.int32, inject.shape, 1)
        low = jnp.where(lane == 0, 0.0, excess_of(inject - pltpu.roll(inject, 1, 1), bound_ref[at, :]))
        high = jnp.where(lane == periods - 1, 0.0, pltpu.roll(low, periods - 1, 1))
        out_ref[at, :] = inject - 0.5 * low + 0.5 * high


def edge_kernel(*refs):
    mine_refs, other_refs, (bound_ref, out_ref) = refs[:chunks], refs[chunks : 2 * chunks], refs[2 * chunks :]
    first = lax.axis_index("tm") == 0
    rows, periods = mine_refs[0].shape
    lane = lax.broadcasted_iota(jnp.int32, (rows, periods), 1)
    at_edge = lane == jnp.where(first, periods - 1, 0)
    sign = jnp.where(first, 0.5, -0.5)
    for c in range(chunks):
        at = pl.ds(c * rows, rows)
        mine, other = mine_refs[c][...], other_refs[c][...]
        other = jnp.where(first, pltpu.roll(other, periods - 1, 1), pltpu.roll(other, 1, 1))
        excess = excess_of(jnp.where(first, other - mine, mine - other), bound_ref[at, :])
        out_ref[at, :] = jnp.where(at_edge, sign * excess, 0.0)


def norms_kernel(entries, left_ref, right_ref, out_ref):
    total = left_ref[...] + right_ref[...]
    row = lax.broadcasted_iota(jnp.int32, total.shape, 0)
    for k in range(passes):
        square = jnp.sum(jnp.where((row >= 3 * k) & (row < 3 * k + 3), total, 0.0), axis=0, keepdims=True)
        out_ref[k] = jnp.sum(jnp.sqrt(jnp.sum(square, axis=1, keepdims=True) / entries))


def squares_kernel(misfit_ref, out_ref):
    misfit = misfit_ref[...]
    out_ref[...] = jnp.sum((misfit * misfit).reshape(-1, 8, misfit.shape[1]), axis=0)


def pack_kernel(*refs):
    *earlier, misfit_ref, out_ref = refs
    misfit = misfit_ref[...]
    sums = [ref[...] for ref in earlier] + [(misfit * misfit).reshape(-1, 8, misfit.shape[1])]
    row = lax.broadcasted_iota(jnp.int32, out_ref.shape, 0)
    out = jnp.zeros(out_ref.shape, jnp.float32)
    for k, value in enumerate(sums):
        left = jnp.sum(value.reshape(-1, misfit.shape[1]), axis=0, keepdims=True)
        for j in range(3):
            piece = left.astype(jnp.bfloat16).astype(jnp.float32)
            out = jnp.where(row == 3 * k + j, piece, out)
            left = left - piece
    out_ref[...] = out.astype(out_ref.dtype)


def unpack_kernel(own_ref, *refs):
    *tiles, out_ref = refs
    tall = own_ref.shape[0]
    total = own_ref[...].astype(jnp.float32)
    for ref in tiles:
        total = total + ref[pl.ds(ref.shape[0] - tall, tall), :].astype(jnp.float32)
    out_ref[...] = total


def limits_of(outage_line, ratings):
    levels = lax.broadcasted_iota(jnp.int32, (outage_line.shape[0], ratings.shape[0]), 1)
    return jnp.sum(jnp.where(outage_line[:, None] == levels, ratings[None, :], 0.0), axis=1)


def project(flows, dual, limits):
    bound = limits[:, None]
    kept = jnp.clip(flows + dual, -bound, bound)
    misfit = flows - kept
    return (misfit, dual + misfit)


def exchanges(axes):
    out = []
    for axis, count in axes:
        if count & (count - 1):
            return None
        out += [(axis, 1 << k) for k in range(count.bit_length() - 1)]
    return out


def total_over(value, axes):
    steps = exchanges([(axis, lax.axis_size(axis)) for axis in axes])
    if steps is None:
        return lax.psum(value, axes)
    for axis, bit in steps:
        value = value + lax.ppermute(value, axis, [(i, i ^ bit) for i in range(lax.axis_size(axis))])
    return value


def beside(block, axis):
    count = lax.axis_size(axis)
    first, last = block[:, :1], block[:, -1:]
    zeros = jnp.zeros_like(first)
    if count == 1:
        return zeros, zeros
    if count == 2:
        at = lax.axis_index(axis)
        other = lax.ppermute(jnp.where(at == 0, last, first), axis, [(0, 1), (1, 0)])
        return jnp.where(at == 0, zeros, other), jnp.where(at == 0, other, zeros)
    low = lax.ppermute(last, axis, [(i, i + 1) for i in range(count - 1)])
    high = lax.ppermute(first, axis, [(i + 1, i) for i in range(count - 1)])
    return low, high


def body(proposal, flow_dual, shift_factors, outage_line, ratings, ramp_limit):
    limits = limits_of(outage_line, ratings)
    owned, periods = proposal.shape
    count = lax.axis_size("net")
    ring = is_ring(count, lax.axis_size("tm"))
    height = owned // chunks
    if ring:
        order = ring_order(count)
        groups = ring_groups(count)
        factors = []
        for part in reorder_parts(groups):
            side = reorder(shift_factors, [d for g in part for d in g], count)
            low = 0
            for g in part:
                factors.append(side[:, low : low + len(g) * owned])
                low += len(g) * owned

    def forward(pieces):
        if not ring:
            whole = lax.all_gather(jnp.concatenate(pieces, axis=0), "net", axis=0, tiled=True)
            return jnp.dot(shift_factors, whole, preferred_element_type=jnp.float32)
        got = ring_gather(pieces, order)
        flows = None
        for group, cols in zip(groups, factors):
            blocks = jnp.concatenate([got[c][d] for d in group for c in range(chunks)], axis=0)
            share = jnp.dot(cols, blocks, preferred_element_type=jnp.float32)
            flows = share if flows is None else flows + share
        return flows

    def backward(misfit, extra):
        narrow = misfit.astype(jnp.bfloat16)
        shares = {}
        for g in reversed(range(len(groups))):
            group, cols = groups[g], factors[g]
            spread = lax.dot_general(cols, narrow, (((0,), (0,)), ((), ())), preferred_element_type=jnp.float32)
            for j, d in enumerate(group):
                for c in range(chunks):
                    shares[c, d] = (spread, j * owned + c * height)
        held, tiles = ring_scatter(lambda c, d: shares[c, d], order, height, extra)
        return [shares[c, 0] for c in range(chunks)], held, tiles

    dual = flow_dual
    sums = []
    entries = float(shift_factors.shape[0] * count * periods * lax.axis_size("tm"))
    if not ring:
        inject = proposal
        for _ in range(passes):
            misfit, dual = project(forward([inject.astype(jnp.bfloat16)]), dual, limits)
            sums.append(jnp.sum(misfit * misfit))
            share = lax.dot_general(
                shift_factors,
                misfit.astype(jnp.bfloat16),
                (((0,), (0,)), ((), ())),
                preferred_element_type=jnp.float32,
            )
            inject = inject - relax_step * lax.psum_scatter(share, "net", scatter_dimension=0, tiled=True)
        norms = jnp.sqrt(total_over(jnp.stack(sums), ("tm", "net")) / entries)
        return (ramp(inject, ramp_limit), dual, norms)

    chunk_shape = jax.ShapeDtypeStruct((height, periods), jnp.bfloat16)
    whole_shape = jax.ShapeDtypeStruct((owned, periods), jnp.float32)
    slim = small_call(narrow_kernel, [chunk_shape] * chunks, proposal)
    inject = proposal
    for stage in range(passes):
        misfit, _ = project(forward(slim), dual, limits)
        dual = small_call(add_kernel, jax.ShapeDtypeStruct(dual.shape, dual.dtype), dual, misfit)
        if stage + 1 < passes:
            tile = jax.ShapeDtypeStruct((8, periods), jnp.float32)
            sums.append(small_call(squares_kernel, tile, misfit))
            extra = None
        else:
            tile = jax.ShapeDtypeStruct((16, periods), jnp.bfloat16)
            extra = small_call(pack_kernel, tile, *sums, misfit)
        own, held, tiles = backward(misfit, extra)
        lows = tuple(low for _, low in own)
        arrived = [held[c, way] for way in (1, -1) for c in range(chunks)]
        if stage + 1 < passes:
            inject, *slim = small_call(
                functools.partial(update_kernel, lows),
                [whole_shape] + [chunk_shape] * chunks,
                own[0][0],
                *arrived,
                inject,
            )
    last, other = [], []
    for c in range(chunks):
        shape = jax.ShapeDtypeStruct((height, periods), jnp.float32)
        kernel = functools.partial(last_update_kernel, own[c][1], c)
        last.append(small_call(kernel, shape, own[c][0], held[c, 1], held[c, -1], inject))
        other.append(lax.ppermute(last[c], "tm", [(0, 1), (1, 0)]))
    bound = jnp.broadcast_to(ramp_limit[:, None], (owned, periods))
    inner = small_call(inner_ramp_kernel, whole_shape, *last, bound)
    wide = jax.ShapeDtypeStruct(extra.shape, jnp.float32)
    sums = small_call(unpack_kernel, wide, extra, *tiles)
    others = lax.ppermute(sums, "tm", [(0, 1), (1, 0)])
    shape = jax.ShapeDtypeStruct((passes,), jnp.float32)
    norms = small_call(functools.partial(norms_kernel, entries), shape, sums, others)
    dispatch = inner + small_call(edge_kernel, whole_shape, *last, *other, bound)
    return (dispatch, dual, norms)


def ramp(inject, ramp_limit):
    periods = inject.shape[1]
    low, high = beside(inject, "tm")
    padded = jnp.concatenate([low, inject, high], axis=1)
    step = padded[:, 1:] - padded[:, :-1]
    bound = ramp_limit[:, None]
    moment = lax.axis_index("tm") * periods + lax.broadcasted_iota(jnp.int32, (1, periods + 1), 1)
    valid = (moment >= 1) & (moment <= periods * lax.axis_size("tm") - 1)
    excess = jnp.where(valid, step - jnp.clip(step, -bound, bound), 0.0)
    return inject - 0.5 * excess[:, :-1] + 0.5 * excess[:, 1:]


def solution(mesh):
    return jax.shard_map(
        body,
        mesh=mesh,
        in_specs=(
            P(("groups", "net"), "tm"),
            P(("groups", "net"), "tm"),
            P("net", None),
            P("net"),
            P(),
            P("net"),
        ),
        out_specs=(P(("groups", "net"), "tm"), P(("groups", "net"), "tm"), P("groups")),
        check_vma=False,
    )
```

```python
import functools

import jax
import jax.numpy as jnp
from jax import lax
from jax.experimental import pallas as pl
from jax.experimental.pallas import tpu as pltpu
from jax.sharding import PartitionSpec as P

relax_step = 0.1
chunks = 2
passes = 2
longest_ring = 8


def is_ring(count, split):
    return 4 <= count <= longest_ring and count % 2 == 0 and split == 2


def ring_order(count):
    return list(range(0, count, 2)) + list(range(count - 1 - count % 2, 0, -2))


def hop_counts(count, chunk):
    far, near = count // 2, (count - 1) // 2
    return (near, far) if chunk % 2 else (far, near)


def gather_sends(count):
    sends = []
    for hop in range(1, count // 2 + 1):
        for flip in (0, 1):
            for chunk in range(chunks):
                for way in (1, -1):
                    limit = hop_counts(count, chunk)[0 if way == 1 else 1]
                    if hop <= limit and (chunk % 2 == (way == -1)) == (flip == 0):
                        sends.append((chunk, way, hop))
    return sends


def scatter_sends(count):
    return gather_sends(count)[::-1]


def hop_to(block, send, order):
    count, split = len(order), lax.axis_size("tm")
    pairs = []
    for t in range(split):
        way = send[1] if t % 2 == 0 else -send[1]
        pairs += [(order[i] * split + t, order[(i + way) % count] * split + t) for i in range(count)]
    return lax.ppermute(block, ("net", "tm"), pairs)


def by_distance(count):
    out = [0]
    for hop in range(1, count // 2 + 1):
        out += [count - hop] if 2 * hop == count else [count - hop, hop]
    return out


def ring_groups(count):
    order = by_distance(count)
    cuts = sorted({0, min(3, count), max(count - 3, min(3, count)), count - 1, count})
    return [order[a:b] for a, b in zip(cuts, cuts[1:])]


def reorder_parts(groups):
    return [[g] for g in groups[:-2]] + [groups[-2:]]


def ring_gather(pieces, order):
    count = len(order)
    got = [{0: p} for p in pieces]
    held = {}
    for send in gather_sends(count):
        chunk, way, hop = send
        block = hop_to(held.get((chunk, way), pieces[chunk]), send, order)
        held[chunk, way] = block
        got[chunk][(-way * hop) % count] = block
    return got


def small_call(kernel, out_shape, *operands):
    touched = sum(x.size * x.dtype.itemsize for x in jax.tree.leaves(out_shape)) * 3
    return pl.pallas_call(
        kernel,
        out_shape=out_shape,
        in_specs=[pl.BlockSpec(memory_space=pltpu.VMEM)] * len(operands),
        out_specs=jax.tree.map(lambda x: pl.BlockSpec(memory_space=pltpu.VMEM if x.ndim > 1 else pltpu.SMEM), out_shape),
        compiler_params=pltpu.CompilerParams(vmem_limit_bytes=16 << 20),
        cost_estimate=pl.CostEstimate(flops=0, transcendentals=0, bytes_accessed=touched),
    )(*operands)


def first_kernel(low, height, spread_ref, *refs):
    out_ref = refs[-1]
    out_ref[pl.ds(0, height), :] = spread_ref[pl.ds(low, height), :].astype(out_ref.dtype)
    if len(refs) > 1:
        out_ref[pl.ds(height, refs[0].shape[0]), :] = refs[0][...]


def add_kernel(left_ref, right_ref, out_ref):
    out_ref[...] = left_ref[...] + right_ref[...]


def sum_kernel(low, height, spread_ref, arrived_ref, out_ref):
    mine = spread_ref[pl.ds(low, height), :]
    top, rest = pl.ds(0, height), out_ref.shape[0] - height
    out_ref[top, :] = (mine + arrived_ref[top, :].astype(jnp.float32)).astype(out_ref.dtype)
    if rest:
        out_ref[pl.ds(height, rest), :] = arrived_ref[pl.ds(height, rest), :]


def update_kernel(lows, spread_ref, *refs):
    ahead, behind, inject_ref, out_ref, slim = refs[:chunks], refs[chunks : 2 * chunks], refs[2 * chunks], refs[2 * chunks + 1], refs[2 * chunks + 2 :]
    height = ahead[0].shape[0]
    for c, low in enumerate(lows):
        rows = pl.ds(c * height, height)
        total = spread_ref[pl.ds(low, height), :]
        total = total + ahead[c][...].astype(jnp.float32) + behind[c][...].astype(jnp.float32)
        inject = inject_ref[rows, :] - relax_step * total
        out_ref[rows, :] = inject
        slim[c][...] = inject.astype(slim[c].dtype)


def ring_scatter(part, order, height, extra=None):
    count = len(order)
    held, tiles = {}, []
    for send in scatter_sends(count):
        chunk, way, hop = send
        spread, low = part(chunk, (way * hop) % count)
        more = extra is not None and chunk == chunks - 1
        rows = height + (extra.shape[0] if more else 0)
        shape = jax.ShapeDtypeStruct((rows, spread.shape[1]), jnp.bfloat16)
        if (chunk, way) in held:
            kernel, tail = sum_kernel, [held[chunk, way]]
        else:
            kernel, tail = first_kernel, [extra] if more else []
        mine = small_call(functools.partial(kernel, low, height), shape, spread, *tail)
        held[chunk, way] = hop_to(mine, send, order)
        if more:
            tiles.append(held[chunk, way])
    return held, tiles


def place_of(position, count):
    return jnp.where(position % 2 == 0, position // 2, count - 1 - position // 2)


def at_place(place, count):
    return jnp.where(place < count // 2, 2 * place, 2 * (count - place) - 1)


def reorder_kernel(distances, count, _, factors_ref, out_ref, sems):
    width = factors_ref.shape[1] // count
    mine = place_of(lax.axis_index("net"), count)
    way = jnp.where(lax.axis_index("tm") % 2 == 0, 1, count - 1)
    copies = []
    for j, distance in enumerate(distances):
        source = at_place((mine + way * distance) % count, count) * width
        copies.append(
            pltpu.make_async_copy(
                factors_ref.at[:, pl.ds(pl.multiple_of(source, width), width)],
                out_ref.at[:, pl.ds(j * width, width)],
                sems.at[j],
            )
        )
    for copy in copies:
        copy.start()
    for copy in copies:
        copy.wait()


def reorder(factors, distances, count):
    rows, width = factors.shape[0], factors.shape[1] // count * len(distances)
    return pl.pallas_call(
        functools.partial(reorder_kernel, tuple(distances), count),
        out_shape=jax.ShapeDtypeStruct((rows, width), factors.dtype),
        in_specs=[pl.BlockSpec(memory_space=pl.ANY), pl.BlockSpec(memory_space=pltpu.HBM)],
        out_specs=pl.BlockSpec(memory_space=pltpu.VMEM),
        scratch_shapes=[pltpu.SemaphoreType.DMA((len(distances),))],
        compiler_params=pltpu.CompilerParams(vmem_limit_bytes=50 << 20),
        cost_estimate=pl.CostEstimate(flops=0, transcendentals=0, bytes_accessed=rows * width * factors.dtype.itemsize),
    )(lax.axis_index("net").reshape(1), factors)


def narrow_kernel(wide_ref, *out_refs):
    height = out_refs[0].shape[0]
    for c, ref in enumerate(out_refs):
        ref[...] = wide_ref[pl.ds(c * height, height), :].astype(ref.dtype)


def last_update_kernel(low, chunk, spread_ref, ahead_ref, behind_ref, inject_ref, out_ref):
    height = out_ref.shape[0]
    top = pl.ds(0, height)
    total = spread_ref[pl.ds(low, height), :]
    total = total + ahead_ref[top, :].astype(jnp.float32) + behind_ref[top, :].astype(jnp.float32)
    out_ref[...] = inject_ref[pl.ds(chunk * height, height), :] - relax_step * total


def excess_of(step, bound):
    return step - jnp.clip(step, -bound, bound)


def inner_ramp_kernel(*refs):
    *parts, bound_ref, out_ref = refs
    for c, ref in enumerate(parts):
        inject = ref[...]
        rows, periods = inject.shape
        at = pl.ds(c * rows, rows)
        lane = lax.broadcasted_iota(jnp.int32, inject.shape, 1)
        low = jnp.where(lane == 0, 0.0, excess_of(inject - pltpu.roll(inject, 1, 1), bound_ref[at, :]))
        high = jnp.where(lane == periods - 1, 0.0, pltpu.roll(low, periods - 1, 1))
        out_ref[at, :] = inject - 0.5 * low + 0.5 * high


def edge_kernel(*refs):
    mine_refs, other_refs, (bound_ref, out_ref) = refs[:chunks], refs[chunks : 2 * chunks], refs[2 * chunks :]
    first = lax.axis_index("tm") == 0
    rows, periods = mine_refs[0].shape
    lane = lax.broadcasted_iota(jnp.int32, (rows, periods), 1)
    at_edge = lane == jnp.where(first, periods - 1, 0)
    sign = jnp.where(first, 0.5, -0.5)
    for c in range(chunks):
        at = pl.ds(c * rows, rows)
        mine, other = mine_refs[c][...], other_refs[c][...]
        other = jnp.where(first, pltpu.roll(other, periods - 1, 1), pltpu.roll(other, 1, 1))
        excess = excess_of(jnp.where(first, other - mine, mine - other), bound_ref[at, :])
        out_ref[at, :] = jnp.where(at_edge, sign * excess, 0.0)


def norms_kernel(entries, left_ref, right_ref, out_ref):
    total = left_ref[...] + right_ref[...]
    row = lax.broadcasted_iota(jnp.int32, total.shape, 0)
    for k in range(passes):
        square = jnp.sum(jnp.where((row >= 3 * k) & (row < 3 * k + 3), total, 0.0), axis=0, keepdims=True)
        out_ref[k] = jnp.sum(jnp.sqrt(jnp.sum(square, axis=1, keepdims=True) / entries))


def squares_kernel(misfit_ref, out_ref):
    misfit = misfit_ref[...]
    out_ref[...] = jnp.sum((misfit * misfit).reshape(-1, 8, misfit.shape[1]), axis=0)


def pack_kernel(*refs):
    *earlier, misfit_ref, out_ref = refs
    misfit = misfit_ref[...]
    sums = [ref[...] for ref in earlier] + [(misfit * misfit).reshape(-1, 8, misfit.shape[1])]
    row = lax.broadcasted_iota(jnp.int32, out_ref.shape, 0)
    out = jnp.zeros(out_ref.shape, jnp.float32)
    for k, value in enumerate(sums):
        left = jnp.sum(value.reshape(-1, misfit.shape[1]), axis=0, keepdims=True)
        for j in range(3):
            piece = left.astype(jnp.bfloat16).astype(jnp.float32)
            out = jnp.where(row == 3 * k + j, piece, out)
            left = left - piece
    out_ref[...] = out.astype(out_ref.dtype)


def unpack_kernel(own_ref, *refs):
    *tiles, out_ref = refs
    tall = own_ref.shape[0]
    total = own_ref[...].astype(jnp.float32)
    for ref in tiles:
        total = total + ref[pl.ds(ref.shape[0] - tall, tall), :].astype(jnp.float32)
    out_ref[...] = total


def limits_of(outage_line, ratings):
    levels = lax.broadcasted_iota(jnp.int32, (outage_line.shape[0], ratings.shape[0]), 1)
    return jnp.sum(jnp.where(outage_line[:, None] == levels, ratings[None, :], 0.0), axis=1)


def project(flows, dual, limits):
    bound = limits[:, None]
    kept = jnp.clip(flows + dual, -bound, bound)
    misfit = flows - kept
    return (misfit, dual + misfit)


def exchanges(axes):
    out = []
    for axis, count in axes:
        if count & (count - 1):
            return None
        out += [(axis, 1 << k) for k in range(count.bit_length() - 1)]
    return out


def total_over(value, axes):
    steps = exchanges([(axis, lax.axis_size(axis)) for axis in axes])
    if steps is None:
        return lax.psum(value, axes)
    for axis, bit in steps:
        value = value + lax.ppermute(value, axis, [(i, i ^ bit) for i in range(lax.axis_size(axis))])
    return value


def beside(block, axis):
    count = lax.axis_size(axis)
    first, last = block[:, :1], block[:, -1:]
    zeros = jnp.zeros_like(first)
    if count == 1:
        return zeros, zeros
    if count == 2:
        at = lax.axis_index(axis)
        other = lax.ppermute(jnp.where(at == 0, last, first), axis, [(0, 1), (1, 0)])
        return jnp.where(at == 0, zeros, other), jnp.where(at == 0, other, zeros)
    low = lax.ppermute(last, axis, [(i, i + 1) for i in range(count - 1)])
    high = lax.ppermute(first, axis, [(i + 1, i) for i in range(count - 1)])
    return low, high


def body(proposal, flow_dual, shift_factors, outage_line, ratings, ramp_limit):
    limits = limits_of(outage_line, ratings)
    owned, periods = proposal.shape
    count = lax.axis_size("net")
    ring = is_ring(count, lax.axis_size("tm"))
    height = owned // chunks
    if ring:
        order = ring_order(count)
        groups = ring_groups(count)
        factors = []
        for part in reorder_parts(groups):
            side = reorder(shift_factors, [d for g in part for d in g], count)
            low = 0
            for g in part:
                factors.append(side[:, low : low + len(g) * owned])
                low += len(g) * owned

    def forward(pieces):
        if not ring:
            whole = lax.all_gather(jnp.concatenate(pieces, axis=0), "net", axis=0, tiled=True)
            return jnp.dot(shift_factors, whole, preferred_element_type=jnp.float32)
        got = ring_gather(pieces, order)
        flows = None
        for group, cols in zip(groups, factors):
            blocks = jnp.concatenate([got[c][d] for d in group for c in range(chunks)], axis=0)
            share = jnp.dot(cols, blocks, preferred_element_type=jnp.float32)
            flows = share if flows is None else flows + share
        return flows

    def backward(misfit, extra):
        narrow = misfit.astype(jnp.bfloat16)
        shares = {}
        for g in reversed(range(len(groups))):
            group, cols = groups[g], factors[g]
            spread = lax.dot_general(cols, narrow, (((0,), (0,)), ((), ())), preferred_element_type=jnp.float32)
            for j, d in enumerate(group):
                for c in range(chunks):
                    shares[c, d] = (spread, j * owned + c * height)
        held, tiles = ring_scatter(lambda c, d: shares[c, d], order, height, extra)
        return [shares[c, 0] for c in range(chunks)], held, tiles

    dual = flow_dual
    sums = []
    entries = float(shift_factors.shape[0] * count * periods * lax.axis_size("tm"))
    if not ring:
        inject = proposal
        for _ in range(passes):
            misfit, dual = project(forward([inject.astype(jnp.bfloat16)]), dual, limits)
            sums.append(jnp.sum(misfit * misfit))
            share = lax.dot_general(
                shift_factors,
                misfit.astype(jnp.bfloat16),
                (((0,), (0,)), ((), ())),
                preferred_element_type=jnp.float32,
            )
            inject = inject - relax_step * lax.psum_scatter(share, "net", scatter_dimension=0, tiled=True)
        norms = jnp.sqrt(total_over(jnp.stack(sums), ("tm", "net")) / entries)
        return (ramp(inject, ramp_limit), dual, norms)

    chunk_shape = jax.ShapeDtypeStruct((height, periods), jnp.bfloat16)
    whole_shape = jax.ShapeDtypeStruct((owned, periods), jnp.float32)
    slim = small_call(narrow_kernel, [chunk_shape] * chunks, proposal)
    inject = proposal
    for stage in range(passes):
        misfit, _ = project(forward(slim), dual, limits)
        dual = small_call(add_kernel, jax.ShapeDtypeStruct(dual.shape, dual.dtype), dual, misfit)
        if stage + 1 < passes:
            tile = jax.ShapeDtypeStruct((8, periods), jnp.float32)
            sums.append(small_call(squares_kernel, tile, misfit))
            extra = None
        else:
            tile = jax.ShapeDtypeStruct((16, periods), jnp.bfloat16)
            extra = small_call(pack_kernel, tile, *sums, misfit)
        own, held, tiles = backward(misfit, extra)
        lows = tuple(low for _, low in own)
        arrived = [held[c, way] for way in (1, -1) for c in range(chunks)]
        if stage + 1 < passes:
            inject, *slim = small_call(
                functools.partial(update_kernel, lows),
                [whole_shape] + [chunk_shape] * chunks,
                own[0][0],
                *arrived,
                inject,
            )
    last, other = [], []
    for c in range(chunks):
        shape = jax.ShapeDtypeStruct((height, periods), jnp.float32)
        kernel = functools.partial(last_update_kernel, own[c][1], c)
        last.append(small_call(kernel, shape, own[c][0], held[c, 1], held[c, -1], inject))
        other.append(lax.ppermute(last[c], "tm", [(0, 1), (1, 0)]))
    bound = jnp.broadcast_to(ramp_limit[:, None], (owned, periods))
    inner = small_call(inner_ramp_kernel, whole_shape, *last, bound)
    wide = jax.ShapeDtypeStruct(extra.shape, jnp.float32)
    sums = small_call(unpack_kernel, wide, extra, *tiles)
    others = lax.ppermute(sums, "tm", [(0, 1), (1, 0)])
    shape = jax.ShapeDtypeStruct((passes,), jnp.float32)
    norms = small_call(functools.partial(norms_kernel, entries), shape, sums, others)
    dispatch = inner + small_call(edge_kernel, whole_shape, *last, *other, bound)
    return (dispatch, dual, norms)


def ramp(inject, ramp_limit):
    periods = inject.shape[1]
    low, high = beside(inject, "tm")
    padded = jnp.concatenate([low, inject, high], axis=1)
    step = padded[:, 1:] - padded[:, :-1]
    bound = ramp_limit[:, None]
    moment = lax.axis_index("tm") * periods + lax.broadcasted_iota(jnp.int32, (1, periods + 1), 1)
    valid = (moment >= 1) & (moment <= periods * lax.axis_size("tm") - 1)
    excess = jnp.where(valid, step - jnp.clip(step, -bound, bound), 0.0)
    return inject - 0.5 * excess[:, :-1] + 0.5 * excess[:, 1:]


def solution(mesh):
    return jax.shard_map(
        body,
        mesh=mesh,
        in_specs=(
            P(("groups", "net"), "tm"),
            P(("groups", "net"), "tm"),
            P("net", None),
            P("net"),
            P(),
            P("net"),
        ),
        out_specs=(P(("groups", "net"), "tm"), P(("groups", "net"), "tm"), P("groups")),
        check_vma=False,
    )
```

```python
import functools

import jax
import jax.numpy as jnp
from jax import lax
from jax.experimental import pallas as pl
from jax.experimental.pallas import tpu as pltpu
from jax.sharding import PartitionSpec as P

relax_step = 0.1
chunks = 2
passes = 2
longest_ring = 8


def is_ring(count, split):
    return 4 <= count <= longest_ring and count % 2 == 0 and split == 2


def ring_order(count):
    return list(range(0, count, 2)) + list(range(count - 1 - count % 2, 0, -2))


def hop_counts(count, chunk):
    far, near = count // 2, (count - 1) // 2
    return (near, far) if chunk % 2 else (far, near)


def hop_order(count, first):
    sends = []
    for hop in range(1, count // 2 + 1):
        for chunk, way in first:
            if hop <= hop_counts(count, chunk)[0 if way == 1 else 1]:
                sends.append((chunk, way, hop))
    return sends


def gather_sends(count):
    return hop_order(count, [(0, 1), (1, -1), (0, -1), (1, 1)])


def scatter_sends(count):
    return hop_order(count, [(0, 1), (1, -1), (1, 1), (0, -1)])[::-1]


def hop_to(block, send, order):
    count, split = len(order), lax.axis_size("tm")
    pairs = []
    for t in range(split):
        way = send[1] if t % 2 == 0 else -send[1]
        pairs += [(order[i] * split + t, order[(i + way) % count] * split + t) for i in range(count)]
    return lax.ppermute(block, ("net", "tm"), pairs)


def by_distance(count):
    out = [0]
    for hop in range(1, count // 2 + 1):
        out += [count - hop] if 2 * hop == count else [count - hop, hop]
    return out


def ring_groups(count):
    order = by_distance(count)
    cuts = sorted({0, min(3, count), max(count - 3, min(3, count)), count - 1, count})
    return [order[a:b] for a, b in zip(cuts, cuts[1:])]


def reorder_parts(groups):
    return [[g] for g in groups[:-2]] + [groups[-2:]]


def ring_gather(pieces, order):
    count = len(order)
    got = [{0: p} for p in pieces]
    held = {}
    for send in gather_sends(count):
        chunk, way, hop = send
        block = hop_to(held.get((chunk, way), pieces[chunk]), send, order)
        held[chunk, way] = block
        got[chunk][(-way * hop) % count] = block
    return got


def small_call(kernel, out_shape, *operands):
    touched = sum(x.size * x.dtype.itemsize for x in jax.tree.leaves(out_shape)) * 3
    return pl.pallas_call(
        kernel,
        out_shape=out_shape,
        in_specs=[pl.BlockSpec(memory_space=pltpu.VMEM)] * len(operands),
        out_specs=jax.tree.map(lambda x: pl.BlockSpec(memory_space=pltpu.VMEM if x.ndim > 1 else pltpu.SMEM), out_shape),
        compiler_params=pltpu.CompilerParams(vmem_limit_bytes=16 << 20),
        cost_estimate=pl.CostEstimate(flops=0, transcendentals=0, bytes_accessed=touched),
    )(*operands)


def first_kernel(low, height, spread_ref, *refs):
    out_ref = refs[-1]
    out_ref[pl.ds(0, height), :] = spread_ref[pl.ds(low, height), :].astype(out_ref.dtype)
    if len(refs) > 1:
        out_ref[pl.ds(height, refs[0].shape[0]), :] = refs[0][...]


def add_kernel(left_ref, right_ref, out_ref):
    out_ref[...] = left_ref[...] + right_ref[...]


def sum_kernel(low, height, spread_ref, arrived_ref, out_ref):
    mine = spread_ref[pl.ds(low, height), :]
    top, rest = pl.ds(0, height), out_ref.shape[0] - height
    out_ref[top, :] = (mine + arrived_ref[top, :].astype(jnp.float32)).astype(out_ref.dtype)
    if rest:
        out_ref[pl.ds(height, rest), :] = arrived_ref[pl.ds(height, rest), :]


def update_kernel(lows, spread_ref, *refs):
    ahead, behind, inject_ref, out_ref, slim = refs[:chunks], refs[chunks : 2 * chunks], refs[2 * chunks], refs[2 * chunks + 1], refs[2 * chunks + 2 :]
    height = ahead[0].shape[0]
    for c, low in enumerate(lows):
        rows = pl.ds(c * height, height)
        total = spread_ref[pl.ds(low, height), :]
        total = total + ahead[c][...].astype(jnp.float32) + behind[c][...].astype(jnp.float32)
        inject = inject_ref[rows, :] - relax_step * total
        out_ref[rows, :] = inject
        slim[c][...] = inject.astype(slim[c].dtype)


def ring_scatter(part, order, height, extra=None):
    count = len(order)
    held, tiles = {}, []
    for send in scatter_sends(count):
        chunk, way, hop = send
        spread, low = part(chunk, (way * hop) % count)
        more = extra is not None and chunk == chunks - 1
        rows = height + (extra.shape[0] if more else 0)
        shape = jax.ShapeDtypeStruct((rows, spread.shape[1]), jnp.bfloat16)
        if (chunk, way) in held:
            kernel, tail = sum_kernel, [held[chunk, way]]
        else:
            kernel, tail = first_kernel, [extra] if more else []
        mine = small_call(functools.partial(kernel, low, height), shape, spread, *tail)
        held[chunk, way] = hop_to(mine, send, order)
        if more:
            tiles.append(held[chunk, way])
    return held, tiles


def place_of(position, count):
    return jnp.where(position % 2 == 0, position // 2, count - 1 - position // 2)


def at_place(place, count):
    return jnp.where(place < count // 2, 2 * place, 2 * (count - place) - 1)


def reorder_kernel(distances, count, _, factors_ref, out_ref, sems):
    width = factors_ref.shape[1] // count
    mine = place_of(lax.axis_index("net"), count)
    way = jnp.where(lax.axis_index("tm") % 2 == 0, 1, count - 1)
    copies = []
    for j, distance in enumerate(distances):
        source = at_place((mine + way * distance) % count, count) * width
        copies.append(
            pltpu.make_async_copy(
                factors_ref.at[:, pl.ds(pl.multiple_of(source, width), width)],
                out_ref.at[:, pl.ds(j * width, width)],
                sems.at[j],
            )
        )
    for copy in copies:
        copy.start()
    for copy in copies:
        copy.wait()


def reorder(factors, distances, count):
    rows, width = factors.shape[0], factors.shape[1] // count * len(distances)
    return pl.pallas_call(
        functools.partial(reorder_kernel, tuple(distances), count),
        out_shape=jax.ShapeDtypeStruct((rows, width), factors.dtype),
        in_specs=[pl.BlockSpec(memory_space=pl.ANY), pl.BlockSpec(memory_space=pltpu.HBM)],
        out_specs=pl.BlockSpec(memory_space=pltpu.VMEM),
        scratch_shapes=[pltpu.SemaphoreType.DMA((len(distances),))],
        compiler_params=pltpu.CompilerParams(vmem_limit_bytes=50 << 20),
        cost_estimate=pl.CostEstimate(flops=0, transcendentals=0, bytes_accessed=rows * width * factors.dtype.itemsize),
    )(lax.axis_index("net").reshape(1), factors)


def narrow_kernel(wide_ref, *out_refs):
    height = out_refs[0].shape[0]
    for c, ref in enumerate(out_refs):
        ref[...] = wide_ref[pl.ds(c * height, height), :].astype(ref.dtype)


def last_update_kernel(low, chunk, spread_ref, ahead_ref, behind_ref, inject_ref, out_ref):
    height = out_ref.shape[0]
    top = pl.ds(0, height)
    total = spread_ref[pl.ds(low, height), :]
    total = total + ahead_ref[top, :].astype(jnp.float32) + behind_ref[top, :].astype(jnp.float32)
    out_ref[...] = inject_ref[pl.ds(chunk * height, height), :] - relax_step * total


def excess_of(step, bound):
    return step - jnp.clip(step, -bound, bound)


def inner_ramp_kernel(*refs):
    *parts, bound_ref, out_ref = refs
    for c, ref in enumerate(parts):
        inject = ref[...]
        rows, periods = inject.shape
        at = pl.ds(c * rows, rows)
        lane = lax.broadcasted_iota(jnp.int32, inject.shape, 1)
        low = jnp.where(lane == 0, 0.0, excess_of(inject - pltpu.roll(inject, 1, 1), bound_ref[at, :]))
        high = jnp.where(lane == periods - 1, 0.0, pltpu.roll(low, periods - 1, 1))
        out_ref[at, :] = inject - 0.5 * low + 0.5 * high


def edge_kernel(*refs):
    mine_refs, other_refs, (bound_ref, out_ref) = refs[:chunks], refs[chunks : 2 * chunks], refs[2 * chunks :]
    first = lax.axis_index("tm") == 0
    rows, periods = mine_refs[0].shape
    lane = lax.broadcasted_iota(jnp.int32, (rows, periods), 1)
    at_edge = lane == jnp.where(first, periods - 1, 0)
    sign = jnp.where(first, 0.5, -0.5)
    for c in range(chunks):
        at = pl.ds(c * rows, rows)
        mine, other = mine_refs[c][...], other_refs[c][...]
        other = jnp.where(first, pltpu.roll(other, periods - 1, 1), pltpu.roll(other, 1, 1))
        excess = excess_of(jnp.where(first, other - mine, mine - other), bound_ref[at, :])
        out_ref[at, :] = jnp.where(at_edge, sign * excess, 0.0)


def norms_kernel(entries, left_ref, right_ref, out_ref):
    total = left_ref[...] + right_ref[...]
    row = lax.broadcasted_iota(jnp.int32, total.shape, 0)
    for k in range(passes):
        square = jnp.sum(jnp.where((row >= 3 * k) & (row < 3 * k + 3), total, 0.0), axis=0, keepdims=True)
        out_ref[k] = jnp.sum(jnp.sqrt(jnp.sum(square, axis=1, keepdims=True) / entries))


def squares_kernel(misfit_ref, out_ref):
    misfit = misfit_ref[...]
    out_ref[...] = jnp.sum((misfit * misfit).reshape(-1, 8, misfit.shape[1]), axis=0)


def pack_kernel(*refs):
    *earlier, misfit_ref, out_ref = refs
    misfit = misfit_ref[...]
    sums = [ref[...] for ref in earlier] + [(misfit * misfit).reshape(-1, 8, misfit.shape[1])]
    row = lax.broadcasted_iota(jnp.int32, out_ref.shape, 0)
    out = jnp.zeros(out_ref.shape, jnp.float32)
    for k, value in enumerate(sums):
        left = jnp.sum(value.reshape(-1, misfit.shape[1]), axis=0, keepdims=True)
        for j in range(3):
            piece = left.astype(jnp.bfloat16).astype(jnp.float32)
            out = jnp.where(row == 3 * k + j, piece, out)
            left = left - piece
    out_ref[...] = out.astype(out_ref.dtype)


def unpack_kernel(own_ref, *refs):
    *tiles, out_ref = refs
    tall = own_ref.shape[0]
    total = own_ref[...].astype(jnp.float32)
    for ref in tiles:
        total = total + ref[pl.ds(ref.shape[0] - tall, tall), :].astype(jnp.float32)
    out_ref[...] = total


def limits_of(outage_line, ratings):
    levels = lax.broadcasted_iota(jnp.int32, (outage_line.shape[0], ratings.shape[0]), 1)
    return jnp.sum(jnp.where(outage_line[:, None] == levels, ratings[None, :], 0.0), axis=1)


def project(flows, dual, limits):
    bound = limits[:, None]
    kept = jnp.clip(flows + dual, -bound, bound)
    misfit = flows - kept
    return (misfit, dual + misfit)


def exchanges(axes):
    out = []
    for axis, count in axes:
        if count & (count - 1):
            return None
        out += [(axis, 1 << k) for k in range(count.bit_length() - 1)]
    return out


def total_over(value, axes):
    steps = exchanges([(axis, lax.axis_size(axis)) for axis in axes])
    if steps is None:
        return lax.psum(value, axes)
    for axis, bit in steps:
        value = value + lax.ppermute(value, axis, [(i, i ^ bit) for i in range(lax.axis_size(axis))])
    return value


def beside(block, axis):
    count = lax.axis_size(axis)
    first, last = block[:, :1], block[:, -1:]
    zeros = jnp.zeros_like(first)
    if count == 1:
        return zeros, zeros
    if count == 2:
        at = lax.axis_index(axis)
        other = lax.ppermute(jnp.where(at == 0, last, first), axis, [(0, 1), (1, 0)])
        return jnp.where(at == 0, zeros, other), jnp.where(at == 0, other, zeros)
    low = lax.ppermute(last, axis, [(i, i + 1) for i in range(count - 1)])
    high = lax.ppermute(first, axis, [(i + 1, i) for i in range(count - 1)])
    return low, high


def body(proposal, flow_dual, shift_factors, outage_line, ratings, ramp_limit):
    limits = limits_of(outage_line, ratings)
    owned, periods = proposal.shape
    count = lax.axis_size("net")
    ring = is_ring(count, lax.axis_size("tm"))
    height = owned // chunks
    if ring:
        order = ring_order(count)
        groups = ring_groups(count)
        factors = []
        for part in reorder_parts(groups):
            side = reorder(shift_factors, [d for g in part for d in g], count)
            low = 0
            for g in part:
                factors.append(side[:, low : low + len(g) * owned])
                low += len(g) * owned

    def forward(pieces):
        if not ring:
            whole = lax.all_gather(jnp.concatenate(pieces, axis=0), "net", axis=0, tiled=True)
            return jnp.dot(shift_factors, whole, preferred_element_type=jnp.float32)
        got = ring_gather(pieces, order)
        flows = None
        for group, cols in zip(groups, factors):
            blocks = jnp.concatenate([got[c][d] for d in group for c in range(chunks)], axis=0)
            share = jnp.dot(cols, blocks, preferred_element_type=jnp.float32)
            flows = share if flows is None else flows + share
        return flows

    def backward(misfit, extra):
        narrow = misfit.astype(jnp.bfloat16)
        shares = {}
        for g in reversed(range(len(groups))):
            group, cols = groups[g], factors[g]
            spread = lax.dot_general(cols, narrow, (((0,), (0,)), ((), ())), preferred_element_type=jnp.float32)
            for j, d in enumerate(group):
                for c in range(chunks):
                    shares[c, d] = (spread, j * owned + c * height)
        held, tiles = ring_scatter(lambda c, d: shares[c, d], order, height, extra)
        return [shares[c, 0] for c in range(chunks)], held, tiles

    dual = flow_dual
    sums = []
    entries = float(shift_factors.shape[0] * count * periods * lax.axis_size("tm"))
    if not ring:
        inject = proposal
        for _ in range(passes):
            misfit, dual = project(forward([inject.astype(jnp.bfloat16)]), dual, limits)
            sums.append(jnp.sum(misfit * misfit))
            share = lax.dot_general(
                shift_factors,
                misfit.astype(jnp.bfloat16),
                (((0,), (0,)), ((), ())),
                preferred_element_type=jnp.float32,
            )
            inject = inject - relax_step * lax.psum_scatter(share, "net", scatter_dimension=0, tiled=True)
        norms = jnp.sqrt(total_over(jnp.stack(sums), ("tm", "net")) / entries)
        return (ramp(inject, ramp_limit), dual, norms)

    chunk_shape = jax.ShapeDtypeStruct((height, periods), jnp.bfloat16)
    whole_shape = jax.ShapeDtypeStruct((owned, periods), jnp.float32)
    slim = small_call(narrow_kernel, [chunk_shape] * chunks, proposal)
    inject = proposal
    for stage in range(passes):
        misfit, _ = project(forward(slim), dual, limits)
        dual = small_call(add_kernel, jax.ShapeDtypeStruct(dual.shape, dual.dtype), dual, misfit)
        if stage + 1 < passes:
            tile = jax.ShapeDtypeStruct((8, periods), jnp.float32)
            sums.append(small_call(squares_kernel, tile, misfit))
            extra = None
        else:
            tile = jax.ShapeDtypeStruct((16, periods), jnp.bfloat16)
            extra = small_call(pack_kernel, tile, *sums, misfit)
        own, held, tiles = backward(misfit, extra)
        lows = tuple(low for _, low in own)
        arrived = [held[c, way] for way in (1, -1) for c in range(chunks)]
        if stage + 1 < passes:
            inject, *slim = small_call(
                functools.partial(update_kernel, lows),
                [whole_shape] + [chunk_shape] * chunks,
                own[0][0],
                *arrived,
                inject,
            )
    last, other = [], []
    for c in range(chunks):
        shape = jax.ShapeDtypeStruct((height, periods), jnp.float32)
        kernel = functools.partial(last_update_kernel, own[c][1], c)
        last.append(small_call(kernel, shape, own[c][0], held[c, 1], held[c, -1], inject))
        other.append(lax.ppermute(last[c], "tm", [(0, 1), (1, 0)]))
    bound = jnp.broadcast_to(ramp_limit[:, None], (owned, periods))
    inner = small_call(inner_ramp_kernel, whole_shape, *last, bound)
    wide = jax.ShapeDtypeStruct(extra.shape, jnp.float32)
    sums = small_call(unpack_kernel, wide, extra, *tiles)
    others = lax.ppermute(sums, "tm", [(0, 1), (1, 0)])
    shape = jax.ShapeDtypeStruct((passes,), jnp.float32)
    norms = small_call(functools.partial(norms_kernel, entries), shape, sums, others)
    dispatch = inner + small_call(edge_kernel, whole_shape, *last, *other, bound)
    return (dispatch, dual, norms)


def ramp(inject, ramp_limit):
    periods = inject.shape[1]
    low, high = beside(inject, "tm")
    padded = jnp.concatenate([low, inject, high], axis=1)
    step = padded[:, 1:] - padded[:, :-1]
    bound = ramp_limit[:, None]
    moment = lax.axis_index("tm") * periods + lax.broadcasted_iota(jnp.int32, (1, periods + 1), 1)
    valid = (moment >= 1) & (moment <= periods * lax.axis_size("tm") - 1)
    excess = jnp.where(valid, step - jnp.clip(step, -bound, bound), 0.0)
    return inject - 0.5 * excess[:, :-1] + 0.5 * excess[:, 1:]


def solution(mesh):
    return jax.shard_map(
        body,
        mesh=mesh,
        in_specs=(
            P(("groups", "net"), "tm"),
            P(("groups", "net"), "tm"),
            P("net", None),
            P("net"),
            P(),
            P("net"),
        ),
        out_specs=(P(("groups", "net"), "tm"), P(("groups", "net"), "tm"), P("groups")),
        check_vma=False,
    )
```
